32 devices in a mesh: groups: 2 (over x), dp: 8 (over z, y), tensor: 2 (over core).
Axes of the slice: x: 2, y: 2, z: 4, core: 2. Of those that a mesh axis runs over, the one named last changes fastest.
Arguments:
- step_input: bfloat16 [1024, 4, 8192], P(('groups', 'dp'), None, 'tensor'), parts along dimension 0, may hold values from -8 to 8
- new_kv: bfloat16 [1024, 4, 2, 1024], P(('groups', 'dp'), None, None, 'tensor'), parts along dimension 0, may hold values from -24 to 24
- resp_cache: bfloat16 [1024, 8, 2, 1024], P(('groups', 'dp'), None, None, 'tensor'), parts along dimension 0, may hold values from -24 to 24
- policy_prompt: bfloat16 [16, 128, 2, 1024], P(('groups', 'dp'), None, None, 'tensor'), parts along dimension 0, may hold values from -24 to 24
- ref_prompt: bfloat16 [16, 128, 2, 1024], P(('groups', 'dp'), None, None, 'tensor'), parts along dimension 0, may hold values from -24 to 24
- prompt_len: int32 [16], P(('groups', 'dp')), parts along dimension 0, may hold values from 1 to 128
- resp_len: int32 [1024], P(('groups', 'dp')), parts along dimension 0, may hold values from 1 to 8
- row_owner: int32 [1024], P(('groups', 'dp')), parts along dimension 0, may hold values from 0 to 7, as said below
- finished: int32 [1024], P(('groups', 'dp')), parts along dimension 0, may hold values 0 or 1
- probe: float32 [8192], P('tensor'), may hold values from -0.12 to 0.12
Outputs:
- decoded: bfloat16 [1024, 4, 8192], P(('groups', 'dp'), None, 'tensor'), parts along dimension 0
- ref_score: float32 [16, 64, 4], P(('groups', 'dp')), parts along dimension 0
The draws below stay inside these ranges and needn't reach their ends.
There are 2 independent parts, one for each index of `groups`. The reference program is written for one: setup_inputs(seed, part) draws one part's arguments, and reference() takes and returns one part's arrays. A program takes and returns all parts, laid end to end along the dimension named above; an argument that names none is the same for every part. Nothing has to cross between parts.
Inputs may be any that keep to these rules, and one draw needn't show every extreme that they name: `row_owner`: among the rows of one block at most 8 name the same owner; in every draw one owner is named by exactly 8 rows of every block.
All inputs are finite; a program needn't handle non-finite values. No bound on the sum of `finished` on one device may be relied on, other than what follows from the above.
Results may differ from the reference program's by a relative error of at most 0.012.
The reference program's roundings to bfloat16 on the way count: a program that leaves them out, or rounds other values in their place, can miss the bound.
Values may be sent and summed in bfloat16 or wider, within the bound.
No kernel may reach another device: no remote copies, remote signals or barrier semaphores. Data moves between devices by JAX's collectives and lax.ppermute only.
A program may use at most 128 MiB of HBM per device.

```python
import math
from functools import partial
import jax
import jax.numpy as jnp
from jax import lax

HQ = 64
KVH = 8
HD = 128
ROWS_DEV = 64
PL = 128
RL = 8
S = 4
CAP = 8
ROWS = 512
N_DP = 8


def kv_block(key, lead_shape, length, salt):
    own_key = jax.random.fold_in(key, salt)
    first_key, second_key = jax.random.split(own_key, 2)
    full_shape = lead_shape + (length, KVH * HD)
    keys_part = jnp.clip(jax.random.normal(first_key, full_shape), -6.0, 6.0)
    values_part = 4.0 * jnp.clip(jax.random.normal(second_key, full_shape), -6.0, 6.0)
    return jnp.stack([keys_part, values_part], axis=-2).astype(jnp.float32)


def draw_policy_prompt(key, part):
    return kv_block(key, (N_DP,), PL, 101).astype(jnp.bfloat16)


def draw_ref_prompt(key, part):
    return kv_block(key, (N_DP,), PL, 102).astype(jnp.bfloat16)


def draw_resp_cache(key, part):
    return kv_block(key, (ROWS_DEV * N_DP,), RL, 103).astype(jnp.bfloat16)


def draw_new_kv(key, part):
    return kv_block(key, (ROWS_DEV * N_DP,), S, 104).astype(jnp.bfloat16)


def draw_step_input(key, part):
    own_key = jax.random.fold_in(key, 105)
    full_shape = (ROWS_DEV * N_DP, S, HQ * HD)
    return jnp.clip(jax.random.normal(own_key, full_shape), -8.0, 8.0).astype(jnp.bfloat16)


def draw_row_owner(key, part):
    own_key = jax.random.fold_in(key, 106)
    busiest = jax.random.randint(jax.random.fold_in(own_key, 1), (), 0, N_DP)
    others = (busiest + 1 + jnp.arange((N_DP - 1) * CAP) // CAP) % N_DP

    def one_block(block_id):
        block_key = jax.random.fold_in(own_key, block_id + 2)
        first_key, second_key = jax.random.split(block_key)
        picked = jax.random.permutation(first_key, others)[:ROWS_DEV - CAP]
        owners = jnp.concatenate([jnp.full((CAP,), busiest, jnp.int32), picked.astype(jnp.int32)])
        return jax.random.permutation(second_key, owners)
    return jax.vmap(one_block)(jnp.arange(N_DP)).reshape(ROWS_DEV * N_DP).astype(jnp.int32)


def draw_resp_len(key, part):
    own_key = jax.random.fold_in(key, 107)
    first_key, second_key = jax.random.split(own_key)
    lengths = jax.random.randint(first_key, (ROWS_DEV * N_DP,), 1, RL + 1)
    longest = jax.random.randint(second_key, (), 0, ROWS_DEV * N_DP)
    return jnp.where(jnp.arange(ROWS_DEV * N_DP) == longest, RL, lengths).astype(jnp.int32)


def draw_prompt_len(key, part):
    own_key = jax.random.fold_in(key, 108)
    first_key, second_key = jax.random.split(own_key)
    lengths = jax.random.randint(first_key, (N_DP,), 1, PL + 1)
    longest = jax.random.randint(second_key, (), 0, N_DP)
    return jnp.where(jnp.arange(N_DP) == longest, PL, lengths).astype(jnp.int32)


def touch_ends(drawn, rng, smallest, high):
    longest = drawn.shape.index(max(drawn.shape))
    spots = []
    for shift in (0, 1):
        where = [jax.random.randint(jax.random.fold_in(rng, axis), (), 0, length) for axis, length in enumerate(drawn.shape)]
        where[longest] = (where[longest] + shift) % drawn.shape[longest]
        spots.append(tuple(where))
    return drawn.at[spots[0]].set(smallest).at[spots[1]].set(high)


def block_scale(stream_key, extent, shards, smallest, top_value):
    def one(dim, parts):
        heights = jax.random.uniform(jax.random.fold_in(jax.random.fold_in(stream_key, 6), dim), (parts,), jnp.float32, smallest / len(shards), top_value / len(shards))
        return jnp.repeat(jnp.exp(heights), extent[dim] // parts).reshape((-1,) + (1,) * (len(extent) - dim - 1))

    level = one(*shards[0])
    for cut in shards[1:]:
        level = level * one(*cut)
    return level


def centred(stream_key, extent, width, reach, cuts=(), held_as=jnp.bfloat16):
    array = width * jax.random.normal(stream_key, extent, jnp.float32)
    if cuts:
        array = array * block_scale(stream_key, extent, cuts, -0.22, 0.18)
    return jnp.clip(array, -reach, reach).astype(held_as)


def setup_inputs(seed: int = 0, part: int = 0) -> dict:
    seeds = jax.random.split(jax.random.key(seed), 11)
    part_keys = jax.random.split(jax.random.fold_in(seeds[10], part), 11)
    return {
        "step_input": draw_step_input(jax.random.fold_in(jax.random.fold_in(seeds[10], part), 71), part),
        "new_kv": draw_new_kv(jax.random.fold_in(jax.random.fold_in(seeds[10], part), 71), part),
        "resp_cache": draw_resp_cache(jax.random.fold_in(jax.random.fold_in(seeds[10], part), 71), part),
        "policy_prompt": draw_policy_prompt(jax.random.fold_in(jax.random.fold_in(seeds[10], part), 71), part),
        "ref_prompt": draw_ref_prompt(jax.random.fold_in(jax.random.fold_in(seeds[10], part), 71), part),
        "prompt_len": draw_prompt_len(jax.random.fold_in(jax.random.fold_in(seeds[10], part), 71), part),
        "resp_len": draw_resp_len(jax.random.fold_in(jax.random.fold_in(seeds[10], part), 71), part),
        "row_owner": draw_row_owner(jax.random.fold_in(jax.random.fold_in(seeds[10], part), 71), part),
        "finished": touch_ends((jax.random.randint(part_keys[8], (ROWS,), 0, 4) < 3).astype(jnp.int32), jax.random.fold_in(part_keys[8], 1), 0, 1),
        "probe": centred(seeds[9], (HQ * HD,), 0.02, 0.12, ((0, 2),), jnp.float32),
    }


def softmax_pieces(scores, key_valid):
    masked = jnp.where(key_valid, scores, -jnp.inf)
    top_score = lax.optimization_barrier(jnp.max(masked, axis=-1, keepdims=True))
    weight = jnp.exp(masked - top_score)
    return (weight, lax.optimization_barrier(jnp.sum(weight, axis=-1)), top_score[..., 0])

def slot_table(row_owner):
    row_count = ROWS_DEV * N_DP
    slot_count = N_DP * CAP
    blocks = row_owner.reshape(N_DP, ROWS_DEV)
    local_iota = jnp.arange(ROWS_DEV)
    earlier = local_iota[None, :] < local_iota[:, None]
    same_owner = (blocks[:, :, None] == blocks[:, None, :]) & earlier[None]
    row_rank = lax.optimization_barrier(jnp.sum(same_owner.astype(jnp.int32), axis=2)).reshape(row_count)
    source = (jnp.arange(row_count) // ROWS_DEV).astype(jnp.int32)
    flat_slot = (row_owner * slot_count + source * CAP + row_rank).astype(jnp.int32)
    table = jnp.full((N_DP * slot_count,), row_count, jnp.int32)
    table = table.at[flat_slot].set(jnp.arange(row_count).astype(jnp.int32))
    return (flat_slot, table.reshape(N_DP, slot_count))

def reference(step_input, new_kv, resp_cache, policy_prompt, ref_prompt, prompt_len, resp_len, row_owner, finished, probe):
    row_count = ROWS_DEV * N_DP
    slot_count = N_DP * CAP
    group_size = HQ // KVH
    q_width = HQ * HD
    kv_width = KVH * HD
    inv_scale = 1.0 / math.sqrt(HD)
    flat_slot, row_of_slot = slot_table(row_owner)
    safe_rows = jnp.minimum(row_of_slot, row_count - 1)
    slot_used = row_of_slot < row_count
    prompt_iota = jnp.arange(PL)
    reply_iota = jnp.arange(RL + S)
    own_all = jnp.concatenate([resp_cache, new_kv], axis=1)
    blocked_all = own_all.reshape(N_DP, ROWS_DEV, RL + S, 2, kv_width)
    blocked_len = resp_len.reshape(N_DP, ROWS_DEV)

    def prompt_part(packed):
        queries, cache_rows, length = packed
        query_heads = queries.astype(jnp.float32).reshape(slot_count, KVH, group_size, HD)
        prompt_keys = cache_rows[:, 0].astype(jnp.float32).reshape(PL, KVH, HD)
        prompt_values = cache_rows[:, 1].astype(jnp.float32).reshape(PL, KVH, HD)
        scores = jnp.einsum('skgd,tkd->skgt', query_heads, prompt_keys) * inv_scale
        weight, weight_sum, top_score = softmax_pieces(scores, prompt_iota < length)
        weight_low = lax.optimization_barrier(weight.astype(jnp.bfloat16)).astype(jnp.float32)
        summed = jnp.einsum('skgt,tkd->skgd', weight_low, prompt_values)
        part_out = (summed / weight_sum[..., None]).astype(jnp.bfloat16).reshape(slot_count, q_width)
        part_lse = (top_score + jnp.log(weight_sum)).reshape(slot_count, HQ)
        return (part_out, part_lse)

    def own_part(step_idx, packed):
        queries, cache_rows, lengths = packed
        query_heads = queries.astype(jnp.float32).reshape(ROWS_DEV, KVH, group_size, HD)
        reply_keys = cache_rows[:, :, 0].astype(jnp.float32).reshape(ROWS_DEV, RL + S, KVH, HD)
        reply_values = cache_rows[:, :, 1].astype(jnp.float32).reshape(ROWS_DEV, RL + S, KVH, HD)
        scores = jnp.einsum('rkgd,rtkd->rkgt', query_heads, reply_keys) * inv_scale
        reply_valid = jnp.where(reply_iota[None, :] < RL, reply_iota[None, :] < lengths[:, None], reply_iota[None, :] <= RL + step_idx)
        weight, weight_sum, top_score = softmax_pieces(scores, reply_valid[:, None, None, :])
        weight_low = lax.optimization_barrier(weight.astype(jnp.bfloat16)).astype(jnp.float32)
        summed = jnp.einsum('rkgt,rtkd->rkgd', weight_low, reply_values)
        own_out = (summed / weight_sum[..., None]).reshape(ROWS_DEV, q_width)
        own_lse = (top_score + jnp.log(weight_sum)).reshape(ROWS_DEV, HQ)
        return (own_out, own_lse)
    previous = jnp.zeros((row_count, q_width), jnp.float32)
    decoded_list = []
    query_list = []
    for step_idx in range(S):
        queries = (step_input[:, step_idx].astype(jnp.float32) + previous).astype(jnp.bfloat16)
        query_list.append(queries)
        slot_queries = jnp.where(slot_used[:, :, None], jnp.take(queries, safe_rows, axis=0), jnp.zeros((), jnp.bfloat16))
        part_out, part_lse = lax.map(prompt_part, (slot_queries, policy_prompt, prompt_len))
        prompt_out = jnp.take(part_out.reshape(N_DP * slot_count, q_width), flat_slot, axis=0).astype(jnp.float32)
        prompt_lse = jnp.take(part_lse.reshape(N_DP * slot_count, HQ), flat_slot, axis=0)
        own_out, own_lse = lax.map(partial(own_part, step_idx), (queries.reshape(N_DP, ROWS_DEV, q_width), blocked_all, blocked_len))
        own_out = own_out.reshape(row_count, HQ, HD)
        own_lse = own_lse.reshape(row_count, HQ)
        joint_lse = jnp.maximum(prompt_lse, own_lse)
        prompt_wt = jnp.exp(prompt_lse - joint_lse)
        own_wt = jnp.exp(own_lse - joint_lse)
        blended = (prompt_wt[..., None] * prompt_out.reshape(row_count, HQ, HD) + own_wt[..., None] * own_out) / (prompt_wt + own_wt)[..., None]
        decoded_now = blended.reshape(row_count, q_width).astype(jnp.bfloat16)
        decoded_list.append(decoded_now)
        previous = lax.optimization_barrier(decoded_now).astype(jnp.float32)
    query_all = jnp.stack(query_list, axis=1)
    live_len = jnp.where(finished == 1, resp_len, 0).astype(jnp.int32)
    probe_heads = probe.reshape(KVH, group_size, HD)

    def score_owner(packed):
        slot_rows, used, cache_rows, length = packed
        slot_len = jnp.where(used, jnp.take(live_len, slot_rows), 0)
        slot_kv = jnp.take(own_all, slot_rows, axis=0).astype(jnp.float32)
        slot_keys = slot_kv[:, :, 0].reshape(slot_count, RL + S, KVH, HD)
        slot_values = slot_kv[:, :, 1].reshape(slot_count, RL + S, KVH, HD)
        slot_queries = jnp.take(query_all, slot_rows, axis=0)
        prompt_keys = cache_rows[:, 0].astype(jnp.float32).reshape(PL, KVH, HD)
        prompt_values = cache_rows[:, 1].astype(jnp.float32).reshape(PL, KVH, HD)
        prompt_valid = jnp.broadcast_to((prompt_iota < length)[None, :], (slot_count, PL))
        columns = []
        for step_idx in range(S):
            query_heads = slot_queries[:, step_idx].astype(jnp.float32).reshape(slot_count, KVH, group_size, HD)
            prompt_scores = jnp.einsum('skgd,tkd->skgt', query_heads, prompt_keys) * inv_scale
            reply_scores = jnp.einsum('skgd,stkd->skgt', query_heads, slot_keys) * inv_scale
            reply_valid = jnp.where(reply_iota[None, :] < RL, reply_iota[None, :] < slot_len[:, None], reply_iota[None, :] <= RL + step_idx)
            key_valid = jnp.concatenate([prompt_valid, reply_valid], axis=1)
            weight, weight_sum, top_score = softmax_pieces(jnp.concatenate([prompt_scores, reply_scores], axis=-1), key_valid[:, None, None, :])
            weight_low = lax.optimization_barrier(weight.astype(jnp.bfloat16)).astype(jnp.float32)
            summed = jnp.einsum('skgt,tkd->skgd', weight_low[..., :PL], prompt_values)
            summed = summed + jnp.einsum('skgt,stkd->skgd', weight_low[..., PL:], slot_values)
            ref_out = summed / weight_sum[..., None]
            columns.append(jnp.einsum('skgd,kgd->s', ref_out, probe_heads, precision=lax.Precision.HIGHEST))
        stacked = jnp.stack(columns, axis=1)
        return jnp.where(slot_len[:, None] > 0, stacked, jnp.zeros((), jnp.float32))
    ref_score = lax.map(score_owner, (safe_rows, slot_used, ref_prompt, prompt_len))
    return (jnp.stack(decoded_list, axis=1), ref_score)
```

```python
import math

import jax
import jax.numpy as jnp
from jax import lax
from jax.experimental import pallas as pl
from jax.experimental.pallas import tpu as pltpu
from jax.sharding import PartitionSpec as P

HD = 128


def softmax_pieces(scores, key_valid):
    masked = jnp.where(key_valid, scores, -jnp.inf)
    top_score = jnp.max(masked, axis=-1, keepdims=True)
    weight = jnp.exp(masked - top_score)
    return (weight, jnp.sum(weight, axis=-1), top_score[..., 0])


def per_device(
    step_input,
    new_kv,
    resp_cache,
    policy_prompt,
    ref_prompt,
    prompt_len,
    resp_len,
    row_owner,
    finished,
    probe,
):
    row_count = step_input.shape[0]
    step_count = step_input.shape[1]
    q_width = step_input.shape[2]
    kv_width = new_kv.shape[3]
    q_heads = q_width // HD
    kv_heads = kv_width // HD
    group_size = q_heads // kv_heads
    inv_scale = 1.0 / math.sqrt(HD)
    peer_count = lax.axis_size("dp")
    capacity = max(2, (row_count + peer_count - 1) // peer_count)
    slot_count = peer_count * capacity
    resp_slots = resp_cache.shape[1]
    prompt_width = policy_prompt.shape[1]
    row_iota = jnp.arange(row_count, dtype=jnp.int32)
    same_owner = (row_owner[:, None] == row_owner[None, :]) & (
        row_iota[None, :] < row_iota[:, None]
    )
    slot_index = row_owner * capacity + jnp.sum(same_owner.astype(jnp.int32), axis=1)
    dispatch = slot_index[:, None] == jnp.arange(slot_count, dtype=jnp.int32)[None, :]
    slot_used = jnp.any(dispatch, axis=0)
    slot_row = jnp.sum(jnp.where(dispatch, row_iota[:, None], 0), axis=0)

    def to_slots(rows_data):
        picked = jnp.take(rows_data, slot_row, axis=0)
        mask_shape = (slot_count,) + (1,) * (rows_data.ndim - 1)
        picked = jnp.where(slot_used.reshape(mask_shape), picked, jnp.zeros_like(picked))
        return picked.reshape((peer_count, capacity) + rows_data.shape[1:])

    live_len = jnp.where(finished == 1, resp_len, 0).astype(jnp.bfloat16)
    own_all = jnp.concatenate([resp_cache, new_kv], axis=1)
    reply_iota = jnp.arange(resp_slots + step_count)
    pol_keys = policy_prompt[0, :, 0].reshape(prompt_width, kv_heads, HD)
    pol_values = policy_prompt[0, :, 1].reshape(prompt_width, kv_heads, HD)
    prompt_valid = jnp.arange(prompt_width) < prompt_len[0]
    resp_keys = own_all[:, :, 0].reshape(row_count, -1, kv_heads, HD)
    resp_values = own_all[:, :, 1].reshape(row_count, -1, kv_heads, HD)
    previous = jnp.zeros((row_count, q_width), jnp.float32)
    decoded_list = []
    query_list = []
    kept_list = []
    for step_idx in range(step_count):
        queries = (step_input[:, step_idx].astype(jnp.float32) + previous).astype(jnp.bfloat16)
        query_list.append(queries)
        received = lax.all_to_all(to_slots(queries), "dp", split_axis=0, concat_axis=0, tiled=True)
        lead_shape = received.shape[:2]
        prompt_queries = received.reshape(-1, kv_heads, group_size, HD)
        scores = (
            jnp.einsum(
                "skgd,tkd->skgt", prompt_queries, pol_keys, preferred_element_type=jnp.float32
            )
            * inv_scale
        )
        prompt_weight, prompt_weight_sum, prompt_top_score = softmax_pieces(scores, prompt_valid)
        prompt_summed = jnp.einsum(
            "skgt,tkd->skgd",
            prompt_weight.astype(jnp.bfloat16),
            pol_values,
            preferred_element_type=jnp.float32,
        )
        part_out = (
            (prompt_summed / prompt_weight_sum[..., None])
            .astype(jnp.bfloat16)
            .reshape(lead_shape + (q_width,))
        )
        part_lse = (prompt_top_score + jnp.log(prompt_weight_sum)).reshape(lead_shape + (q_heads,))
        back_out = lax.all_to_all(part_out, "dp", split_axis=0, concat_axis=0, tiled=True)
        back_lse = lax.all_to_all(part_lse, "dp", split_axis=0, concat_axis=0, tiled=True)
        results = (back_out, back_lse, received)
        back_out = results[0]
        back_lse = results[1]
        kept_list.append(results[2])
        prompt_out = jnp.take(back_out.reshape(slot_count, q_width), slot_index, axis=0).astype(
            jnp.float32
        )
        prompt_lse = jnp.take(back_lse.reshape(slot_count, q_heads), slot_index, axis=0)
        query_heads = queries.reshape(row_count, kv_heads, group_size, HD)
        scores = (
            jnp.einsum(
                "rkgd,rtkd->rkgt", query_heads, resp_keys, preferred_element_type=jnp.float32
            )
            * inv_scale
        )
        reply_valid = jnp.where(
            reply_iota[None, :] < resp_slots,
            reply_iota[None, :] < resp_len[:, None],
            reply_iota[None, :] <= resp_slots + step_idx,
        )
        weight, weight_sum, top_score = softmax_pieces(scores, reply_valid[:, None, None, :])
        summed = jnp.einsum(
            "rkgt,rtkd->rkgd",
            weight.astype(jnp.bfloat16),
            resp_values,
            preferred_element_type=jnp.float32,
        )
        own_out = (summed / weight_sum[..., None]).reshape(row_count, q_heads, HD)
        own_lse = (top_score + jnp.log(weight_sum)).reshape(row_count, q_heads)
        joint_lse = jnp.maximum(prompt_lse, own_lse)
        prompt_wt = jnp.exp(prompt_lse - joint_lse)
        own_wt = jnp.exp(own_lse - joint_lse)
        blended = (
            prompt_wt[..., None] * prompt_out.reshape(row_count, q_heads, HD)
            + own_wt[..., None] * own_out
        ) / (prompt_wt + own_wt)[..., None]
        decoded_now = blended.reshape(row_count, q_width).astype(jnp.bfloat16)
        decoded_list.append(decoded_now)
        previous = lax.optimization_barrier(decoded_now).astype(jnp.float32)
    recv_kv, recv_live = (
        lax.all_to_all(to_slots(own_all), "dp", split_axis=0, concat_axis=0, tiled=True),
        lax.all_to_all(to_slots(live_len), "dp", split_axis=0, concat_axis=0, tiled=True),
    )
    recv_queries = jnp.stack(kept_list, axis=2)
    ref_keys = ref_prompt[0, :, 0].reshape(prompt_width, kv_heads, HD)
    ref_values = ref_prompt[0, :, 1].reshape(prompt_width, kv_heads, HD)
    slot_kv = recv_kv.reshape(slot_count, resp_slots + step_count, 2, kv_width)
    slot_keys = slot_kv[:, :, 0].reshape(slot_count, -1, kv_heads, HD)
    slot_values = slot_kv[:, :, 1].reshape(slot_count, -1, kv_heads, HD)
    slot_len = recv_live.reshape(slot_count).astype(jnp.int32)
    slot_queries = recv_queries.reshape(slot_count, step_count, q_width)
    probe_heads = probe.reshape(kv_heads, group_size, HD)
    prompt_mask = jnp.broadcast_to(prompt_valid[None, :], (slot_count, prompt_width))
    score_list = []
    for step_idx in range(step_count):
        queries = slot_queries[:, step_idx].reshape(slot_count, kv_heads, group_size, HD)
        prompt_scores = (
            jnp.einsum("skgd,tkd->skgt", queries, ref_keys, preferred_element_type=jnp.float32)
            * inv_scale
        )
        reply_scores = (
            jnp.einsum("skgd,stkd->skgt", queries, slot_keys, preferred_element_type=jnp.float32)
            * inv_scale
        )
        reply_valid = jnp.where(
            reply_iota[None, :] < resp_slots,
            reply_iota[None, :] < slot_len[:, None],
            reply_iota[None, :] <= resp_slots + step_idx,
        )
        key_valid = jnp.concatenate([prompt_mask, reply_valid], axis=1)
        weight, weight_sum, top_score = softmax_pieces(
            jnp.concatenate([prompt_scores, reply_scores], axis=-1), key_valid[:, None, None, :]
        )
        weight_low = weight.astype(jnp.bfloat16)
        summed = jnp.einsum(
            "skgt,tkd->skgd",
            weight_low[..., :prompt_width],
            ref_values,
            preferred_element_type=jnp.float32,
        )
        summed = summed + jnp.einsum(
            "skgt,stkd->skgd",
            weight_low[..., prompt_width:],
            slot_values,
            preferred_element_type=jnp.float32,
        )
        ref_out = summed / weight_sum[..., None]
        score_list.append(
            jnp.einsum("skgd,kgd->s", ref_out, probe_heads, precision=lax.Precision.HIGHEST)
        )
    head_terms = jnp.stack(score_list, axis=1)
    head_total = lax.psum(head_terms, "tensor")
    ref_score = jnp.where(slot_len[:, None] > 0, head_total, jnp.zeros((), jnp.float32)).reshape(
        1, slot_count, step_count
    )
    return (jnp.stack(decoded_list, axis=1), ref_score)


def ring_order(count):
    return list(range(0, count, 2)) + list(range(count - 1, 0, -2))


def slot_table_kernel(owner_ref, len_ref, fin_ref, rows_ref, lens_ref, live_ref, count_ref):
    peers = count_ref.shape[0]
    slots = rows_ref.shape[0]
    capacity = slots // peers

    def clear(i, c):
        rows_ref[i] = -1
        lens_ref[i] = 1
        live_ref[i] = 0
        return c

    lax.fori_loop(0, slots, clear, 0)
    for o in range(peers):
        count_ref[o] = 0

    def place(r, c):
        o = jnp.clip(owner_ref[r], 0, peers - 1)
        k = count_ref[o]
        at = o * capacity + jnp.minimum(k, capacity - 1)
        rows_ref[at] = r
        lens_ref[at] = len_ref[r]
        live_ref[at] = fin_ref[r]
        count_ref[o] = k + 1
        return c

    lax.fori_loop(0, owner_ref.shape[0], place, 0)


def slot_tables(row_owner, resp_len, finished, peers, capacity):
    smem = pl.BlockSpec(memory_space=pltpu.SMEM)
    shape = jax.ShapeDtypeStruct((peers * capacity,), jnp.int32)
    return pl.pallas_call(
        slot_table_kernel,
        in_specs=[smem] * 3,
        out_specs=[smem] * 3,
        out_shape=[shape] * 3,
        scratch_shapes=[pltpu.SMEM((peers,), jnp.int32)],
        name="slots",
    )(row_owner, resp_len, finished)


def iota(shape, dim):
    return lax.broadcasted_iota(jnp.int32, shape, dim)


def split_matrix(pairs):
    i = iota((2 * pairs, 2 * pairs), 0)
    j = iota((2 * pairs, 2 * pairs), 1)
    src = jnp.where(i < pairs, 2 * i, 2 * (i - pairs) + 1)
    return jnp.where(src == j, 1.0, 0.0).astype(jnp.bfloat16)


def swap_matrix(outer, inner):
    n = outer * inner
    i = iota((n, n), 0)
    j = iota((n, n), 1)
    src = (i % outer) * inner + i // outer
    return jnp.where(src == j, 1.0, 0.0).astype(jnp.bfloat16)


def mm(a, b):
    return jnp.dot(a, b, preferred_element_type=jnp.float32)


def mm_t(a, b):
    return lax.dot_general(a, b, (((1,), (1,)), ((), ())), preferred_element_type=jnp.float32)


def own_masks(lens_ref, base, rows, old, steps, width):
    lane = iota((rows, width), 1)
    sub = iota((rows, width), 0)
    split = rows * old
    is_old = lane < split
    key_row = jnp.where(is_old, lane // old, (lane - split) // steps)
    key_pos = jnp.where(is_old, lane % old, (lane - split) % steps)
    limit = jnp.zeros((rows, width), jnp.int32)
    for k in range(rows):
        limit = jnp.where(sub == k, lens_ref[base + k], limit)
    mine = (key_row == sub) & (lane < rows * (old + steps))
    return [
        mine & (key_pos < jnp.where(is_old, limit, step_idx + 1)) for step_idx in range(steps)
    ]


def make_decode(pieces, first, capacity, steps, old, kv_heads, group):
    head_rows = group * capacity
    inv_scale = 1.0 / math.sqrt(HD)

    def body(*refs):
        place_ref, plen_ref, rows_ref, lens_ref = refs[:4]
        x_hbm, rc_hbm, nk_hbm = refs[4:7]
        prompts = refs[7 : 7 + pieces]
        at = 7 + pieces + (0 if first else 1)
        dec_hbm, q_ref, ko_ref, vo_ref = refs[at : at + 4]
        xbuf, rcbuf, nkbuf, obuf, xs, kc, vp, insem, outsem = refs[at + 4 :]
        width = prompts[0].shape[1]
        kv_width = kv_heads * HD

        def owner(p):
            return place_ref[p]

        def loads(p):
            out = []
            for k in range(capacity):
                row = jnp.maximum(rows_ref[owner(p) * capacity + k], 0)
                out += [
                    pltpu.make_async_copy(x_hbm.at[row], xbuf.at[p, k], insem.at[p, k, 0]),
                    pltpu.make_async_copy(rc_hbm.at[row], rcbuf.at[p, k], insem.at[p, k, 1]),
                    pltpu.make_async_copy(nk_hbm.at[row], nkbuf.at[p, k], insem.at[p, k, 2]),
                ]
            return out

        flights = [loads(p) for p in range(pieces)]
        for f in flights:
            for c in f:
                c.start()
        split_p = split_matrix(width)
        split_rc = split_matrix(capacity * old)
        split_nk = split_matrix(capacity * steps)
        to_steps = swap_matrix(capacity, steps)
        to_rows = swap_matrix(steps, capacity)
        pad = width - capacity * (old + steps)
        for p in range(pieces):
            both = mm(split_p, prompts[p][0].reshape(2 * width, kv_width)).astype(jnp.bfloat16)
            kc[p, :width] = both[:width]
            vp[p] = both[width:]
        for p in range(pieces):
            for c in flights[p]:
                c.wait()
            rc = mm(split_rc, rcbuf[p].reshape(2 * capacity * old, kv_width))
            nk = mm(split_nk, nkbuf[p].reshape(2 * capacity * steps, kv_width))
            n_old, n_new = capacity * old, capacity * steps
            zero = jnp.zeros((pad, kv_width), jnp.float32)
            ko = jnp.concatenate([rc[:n_old], nk[:n_new], zero], 0).astype(jnp.bfloat16)
            vo = jnp.concatenate([rc[n_old:], nk[n_new:], zero], 0).astype(jnp.bfloat16)
            kc[p, width:] = ko
            ko_ref[p] = ko
            vo_ref[p] = vo
            xs[p] = mm(to_steps, xbuf[p].reshape(capacity * steps, -1))
        masks = [
            own_masks(lens_ref, owner(p) * capacity, capacity, old, steps, width)
            for p in range(pieces)
        ]
        lane = iota((head_rows, width), 1)
        pmask = [lane < plen_ref[owner(p) if not first else 0] for p in range(pieces)]
        prev = [[None] * kv_heads for _ in range(pieces)]
        done = [[None] * steps for _ in range(pieces)]
        for s in range(steps):
            for p in range(pieces):
                omask = jnp.concatenate([masks[p][s]] * group, 0)
                parts = []
                for g in range(kv_heads):
                    cols = [
                        xs[p, s * capacity : (s + 1) * capacity, (g * group + h) * HD : (g * group + h + 1) * HD]
                        for h in range(group)
                    ]
                    q = jnp.concatenate(cols, 0)
                    if s > 0:
                        q = q + prev[p][g]
                    q = q.astype(jnp.bfloat16)
                    q_ref[p, g, s * head_rows : (s + 1) * head_rows] = q
                    z = mm_t(q, kc[p, :, g * HD : (g + 1) * HD]) * inv_scale
                    zp = jnp.where(pmask[p], z[:, :width], -jnp.inf)
                    zo = jnp.where(omask, z[:, width:], -jnp.inf)
                    top_p = jnp.max(zp, axis=1, keepdims=True)
                    top_o = jnp.max(zo, axis=1, keepdims=True)
                    wp = jnp.exp(zp - top_p)
                    wo = jnp.exp(zo - top_o)
                    lp = jnp.sum(wp, axis=1, keepdims=True)
                    lo = jnp.sum(wo, axis=1, keepdims=True)
                    accp = mm(wp.astype(jnp.bfloat16), vp[p, :, g * HD : (g + 1) * HD])
                    acco = mm(wo.astype(jnp.bfloat16), vo_ref[p, :, g * HD : (g + 1) * HD])
                    out_p = (accp / lp).astype(jnp.bfloat16).astype(jnp.float32)
                    lse_p = top_p + jnp.log(lp)
                    lse_o = top_o + jnp.log(lo)
                    top = jnp.maximum(lse_p, lse_o)
                    a = jnp.exp(lse_p - top)
                    c = jnp.exp(lse_o - top)
                    inv = 1.0 / (a + c)
                    mix = out_p * (a * inv) + acco * (c * inv / lo)
                    mix = mix.astype(jnp.bfloat16).astype(jnp.float32)
                    prev[p][g] = mix
                    parts += [mix[h * capacity : (h + 1) * capacity] for h in range(group)]
                done[p][s] = jnp.concatenate(parts, 1)
        for p in range(pieces):
            d = jnp.concatenate(done[p], 0).astype(jnp.bfloat16)
            obuf[p] = mm(to_rows, d).astype(jnp.bfloat16).reshape(obuf.shape[1:])
            for k in range(capacity):
                row = rows_ref[owner(p) * capacity + k]

                @pl.when(row >= 0)
                def _():
                    pltpu.make_async_copy(obuf.at[p, k], dec_hbm.at[row], outsem.at[p, k]).start()

        for p in range(pieces):
            for k in range(capacity):
                row = rows_ref[owner(p) * capacity + k]

                @pl.when(row >= 0)
                def _():
                    pltpu.make_async_copy(obuf.at[p, k], dec_hbm.at[row], outsem.at[p, k]).wait()

    return body


def decode_pieces(places, plen, rows, lens, x, rc, nk, prompts, dec, capacity, first):
    pieces = len(prompts)
    count, steps, q_width = x.shape
    old = rc.shape[1]
    kv_width = rc.shape[3]
    kv_heads = kv_width // HD
    group = q_width // kv_width
    width = prompts[0].shape[1]
    body = make_decode(pieces, first, capacity, steps, old, kv_heads, group)
    smem = pl.BlockSpec(memory_space=pltpu.SMEM)
    vmem = pl.BlockSpec(memory_space=pltpu.VMEM)
    anyspec = pl.BlockSpec(memory_space=pl.ANY)
    args = [places, plen, rows, lens, x, rc, nk, *prompts]
    specs = [smem] * 4 + [anyspec] * 3 + [vmem] * pieces
    if not first:
        args.append(dec)
        specs.append(anyspec)
    bf = jnp.bfloat16
    return pl.pallas_call(
        body,
        in_specs=specs,
        out_specs=[anyspec, vmem, vmem, vmem],
        out_shape=[
            jax.ShapeDtypeStruct(x.shape, bf),
            jax.ShapeDtypeStruct((pieces, kv_heads, steps * group * capacity, HD), bf),
            jax.ShapeDtypeStruct((pieces, width, kv_width), bf),
            jax.ShapeDtypeStruct((pieces, width, kv_width), bf),
        ],
        scratch_shapes=[
            pltpu.VMEM((pieces, capacity, steps, q_width), bf),
            pltpu.VMEM((pieces, capacity, old, 2, kv_width), bf),
            pltpu.VMEM((pieces, capacity, steps, 2, kv_width), bf),
            pltpu.VMEM((pieces, capacity, steps, q_width), bf),
            pltpu.VMEM((pieces, capacity * steps, q_width), jnp.float32),
            pltpu.VMEM((pieces, 2 * width, kv_width), bf),
            pltpu.VMEM((pieces, width, kv_width), bf),
            pltpu.SemaphoreType.DMA((pieces, capacity, 3)),
            pltpu.SemaphoreType.DMA((pieces, capacity)),
        ],
        input_output_aliases={} if first else {len(args) - 1: 0},
        compiler_params=pltpu.CompilerParams(vmem_limit_bytes=24 << 20),
        name="decode",
    )(*args)


def make_score(pieces, first, capacity, steps, old, kv_heads, group):
    head_rows = group * capacity
    inv_scale = 1.0 / math.sqrt(HD)

    def body(*refs):
        place_ref, plen_ref, lens_ref, live_ref, block_ref = refs[:5]
        q_ref, ko_ref, vo_ref, probe_ref = refs[5:9]
        prompts = refs[9 : 9 + pieces]
        out_ref, kc, vc = refs[9 + pieces :]
        width = prompts[0].shape[1]
        kv_width = kv_heads * HD
        split_p = split_matrix(width)
        lane = iota((head_rows, width), 1)
        out_lane = iota((capacity, HD), 1)
        out_sub = iota((capacity, HD), 0)
        for p in range(pieces):
            own = place_ref[p]
            both = mm(split_p, prompts[p][0].reshape(2 * width, kv_width)).astype(jnp.bfloat16)
            kc[p, :width] = both[:width]
            vc[p, :width] = both[width:]
            kc[p, width:] = ko_ref[p]
            vc[p, width:] = vo_ref[p]
            pmask = lane < plen_ref[own if not first else 0]
            masks = own_masks(lens_ref, own * capacity, capacity, old, steps, width)
            full = jnp.concatenate(
                [
                    jnp.concatenate([pmask, jnp.concatenate([masks[s]] * group, 0)], 1)
                    for s in range(steps)
                ],
                0,
            )
            total = [jnp.zeros((capacity, HD), jnp.float32) for _ in range(steps)]
            for g in range(kv_heads):
                z = mm_t(q_ref[p, g], kc[p, :, g * HD : (g + 1) * HD]) * inv_scale
                z = jnp.where(full, z, -jnp.inf)
                w = jnp.exp(z - jnp.max(z, axis=1, keepdims=True))
                acc = mm(w.astype(jnp.bfloat16), vc[p, :, g * HD : (g + 1) * HD])
                acc = acc / jnp.sum(w, axis=1, keepdims=True)
                for s in range(steps):
                    for h in range(group):
                        lo = (s * group + h) * capacity
                        weight = probe_ref[g * group + h : g * group + h + 1, :]
                        total[s] = total[s] + acc[lo : lo + capacity] * weight
            live = jnp.zeros((capacity, HD), jnp.int32)
            for k in range(capacity):
                live = jnp.where(out_sub == k, live_ref[own * capacity + k], live)
            here = (out_lane == block_ref[0] * capacity + out_sub) & (live == 1)
            for s in range(steps):
                value = jnp.sum(total[s], axis=1, keepdims=True)
                out_ref[p, s : s + 1, :] = jnp.sum(
                    jnp.where(here, value, 0.0), axis=0, keepdims=True
                )

    return body


def score_pieces(places, plen, lens, live, block, q, ko, vo, probe, prompts, capacity, steps, old, first):
    pieces = len(prompts)
    kv_heads = q.shape[1]
    group = q.shape[2] // (steps * capacity)
    width = prompts[0].shape[1]
    kv_width = kv_heads * HD
    body = make_score(pieces, first, capacity, steps, old, kv_heads, group)
    smem = pl.BlockSpec(memory_space=pltpu.SMEM)
    vmem = pl.BlockSpec(memory_space=pltpu.VMEM)
    bf = jnp.bfloat16
    return pl.pallas_call(
        body,
        in_specs=[smem] * 5 + [vmem] * (4 + pieces),
        out_specs=vmem,
        out_shape=jax.ShapeDtypeStruct((pieces, steps, HD), jnp.float32),
        scratch_shapes=[
            pltpu.VMEM((pieces, 2 * width, kv_width), bf),
            pltpu.VMEM((pieces, 2 * width, kv_width), bf),
        ],
        compiler_params=pltpu.CompilerParams(vmem_limit_bytes=24 << 20),
        name="score",
    )(places, plen, lens, live, block, q, ko, vo, probe, *prompts)


def gather_kernel(*refs):
    place_ref = refs[0]
    parts = refs[1:-1]
    out_ref = refs[-1]
    n = 0
    for part in parts:
        for p in range(part.shape[0]):
            for t in range(out_ref.shape[1]):
                out_ref[place_ref[n], t] = part[p]
            n += 1


def ring_fits(step_input, new_kv, resp_cache, policy_prompt, *rest):
    peers = lax.axis_size("dp")
    row_count, step_count, q_width = step_input.shape
    old = resp_cache.shape[1]
    kv_width = new_kv.shape[3]
    width = policy_prompt.shape[1]
    capacity = max(2, (row_count + peers - 1) // peers)
    gathered = 2 * peers * policy_prompt.size
    exchanged = 2 * step_input.size + new_kv.size + resp_cache.size
    return (
        gathered <= exchanged
        and peers % 2 == 0
        and peers >= 4
        and capacity % 8 == 0
        and peers * capacity <= HD
        and capacity * (old + step_count) <= width
        and width % HD == 0
        and q_width % kv_width == 0
    )


def per_device_ring(
    step_input,
    new_kv,
    resp_cache,
    policy_prompt,
    ref_prompt,
    prompt_len,
    resp_len,
    row_owner,
    finished,
    probe,
):
    row_count, step_count, q_width = step_input.shape
    peers = lax.axis_size("dp")
    halves = lax.axis_size("tensor")
    capacity = max(2, (row_count + peers - 1) // peers)
    old = resp_cache.shape[1]
    me = lax.axis_index("dp")
    ring = ring_order(peers)
    forward = [(ring[i], ring[(i + 1) % peers]) for i in range(peers)]
    backward = [(b, a) for a, b in forward]
    spot = {d: i for i, d in enumerate(ring)}
    offsets = [0]
    for d in range(1, peers // 2):
        offsets += [-d, d]
    offsets.append(peers // 2)
    table = [[ring[(spot[dev] + off) % peers] for off in offsets] for dev in range(peers)]
    places = jnp.take(jnp.array(table, jnp.int32), me, axis=0)
    block = me.astype(jnp.int32).reshape(1)
    rows, lens, live = slot_tables(row_owner, resp_len, finished, peers, capacity)
    plen_all = lax.all_to_all(
        jnp.broadcast_to(prompt_len, (peers,)), "dp", split_axis=0, concat_axis=0, tiled=True
    )
    probe_heads = probe.reshape(q_width // HD, HD)
    dec = None
    scores = []

    def work(pol, ref, begin, dec):
        first = begin == 0
        at = places[begin : begin + len(pol)]
        plen = prompt_len if first else plen_all
        dec, q, ko, vo = decode_pieces(
            at, plen, rows, lens, step_input, resp_cache, new_kv, pol, dec, capacity, first
        )
        scores.append(
            score_pieces(
                at, plen, lens, live, block, q, ko, vo, probe_heads, ref, capacity, step_count, old, first
            )
        )
        return dec

    dec = work([policy_prompt], [ref_prompt], 0, dec)
    pf = pb = policy_prompt
    rf = rb = ref_prompt
    begin = 1
    for d in range(1, peers // 2):
        pf = lax.ppermute(pf, "dp", forward)
        pb = lax.ppermute(pb, "dp", backward)
        rf = lax.ppermute(rf, "dp", forward)
        rb = lax.ppermute(rb, "dp", backward)
        dec = work([pf, pb], [rf, rb], begin, dec)
        begin += 2
    pf = lax.ppermute(pf, "dp", forward)
    rb = lax.ppermute(rb, "dp", backward)
    dec = work([pf], [rb], begin, dec)
    vmem = pl.BlockSpec(memory_space=pltpu.VMEM)
    send = pl.pallas_call(
        gather_kernel,
        in_specs=[pl.BlockSpec(memory_space=pltpu.SMEM)] + [vmem] * len(scores),
        out_specs=vmem,
        out_shape=jax.ShapeDtypeStruct((peers, halves, step_count, HD), jnp.float32),
        name="collect",
    )(places, *scores)
    got = lax.all_to_all(
        send.reshape(peers * halves, step_count, HD),
        ("dp", "tensor"),
        split_axis=0,
        concat_axis=0,
        tiled=True,
    )
    total = jnp.sum(got, axis=0)[:, : peers * capacity]
    return dec, total.T.reshape(1, peers * capacity, step_count)


def solution(mesh):
    in_specs = (
        P(("groups", "dp"), None, "tensor"),
        P(("groups", "dp"), None, None, "tensor"),
        P(("groups", "dp"), None, None, "tensor"),
        P(("groups", "dp"), None, None, "tensor"),
        P(("groups", "dp"), None, None, "tensor"),
        P(("groups", "dp")),
        P(("groups", "dp")),
        P(("groups", "dp")),
        P(("groups", "dp")),
        P("tensor"),
    )
    out_specs = (P(("groups", "dp"), None, "tensor"), P(("groups", "dp"), None, None))

    def run(step_input, new_kv, resp_cache, *rest):
        args = (step_input, new_kv, resp_cache, *rest)
        pick = per_device_ring if ring_fits(*args) else per_device
        return pick(*args)

    return jax.shard_map(
        run, mesh=mesh, in_specs=in_specs, out_specs=out_specs, check_vma=False
    )
```

```python
import math

import jax
import jax.numpy as jnp
from jax import lax
from jax.experimental import pallas as pl
from jax.experimental.pallas import tpu as pltpu
from jax.sharding import PartitionSpec as P

HD = 128


def softmax_pieces(scores, key_valid):
    masked = jnp.where(key_valid, scores, -jnp.inf)
    top_score = jnp.max(masked, axis=-1, keepdims=True)
    weight = jnp.exp(masked - top_score)
    return (weight, jnp.sum(weight, axis=-1), top_score[..., 0])


def per_device(
    step_input,
    new_kv,
    resp_cache,
    policy_prompt,
    ref_prompt,
    prompt_len,
    resp_len,
    row_owner,
    finished,
    probe,
):
    row_count = step_input.shape[0]
    step_count = step_input.shape[1]
    q_width = step_input.shape[2]
    kv_width = new_kv.shape[3]
    q_heads = q_width // HD
    kv_heads = kv_width // HD
    group_size = q_heads // kv_heads
    inv_scale = 1.0 / math.sqrt(HD)
    peer_count = lax.axis_size("dp")
    capacity = max(2, (row_count + peer_count - 1) // peer_count)
    slot_count = peer_count * capacity
    resp_slots = resp_cache.shape[1]
    prompt_width = policy_prompt.shape[1]
    row_iota = jnp.arange(row_count, dtype=jnp.int32)
    same_owner = (row_owner[:, None] == row_owner[None, :]) & (
        row_iota[None, :] < row_iota[:, None]
    )
    slot_index = row_owner * capacity + jnp.sum(same_owner.astype(jnp.int32), axis=1)
    dispatch = slot_index[:, None] == jnp.arange(slot_count, dtype=jnp.int32)[None, :]
    slot_used = jnp.any(dispatch, axis=0)
    slot_row = jnp.sum(jnp.where(dispatch, row_iota[:, None], 0), axis=0)

    def to_slots(rows_data):
        picked = jnp.take(rows_data, slot_row, axis=0)
        mask_shape = (slot_count,) + (1,) * (rows_data.ndim - 1)
        picked = jnp.where(slot_used.reshape(mask_shape), picked, jnp.zeros_like(picked))
        return picked.reshape((peer_count, capacity) + rows_data.shape[1:])

    live_len = jnp.where(finished == 1, resp_len, 0).astype(jnp.bfloat16)
    own_all = jnp.concatenate([resp_cache, new_kv], axis=1)
    reply_iota = jnp.arange(resp_slots + step_count)
    pol_keys = policy_prompt[0, :, 0].reshape(prompt_width, kv_heads, HD)
    pol_values = policy_prompt[0, :, 1].reshape(prompt_width, kv_heads, HD)
    prompt_valid = jnp.arange(prompt_width) < prompt_len[0]
    resp_keys = own_all[:, :, 0].reshape(row_count, -1, kv_heads, HD)
    resp_values = own_all[:, :, 1].reshape(row_count, -1, kv_heads, HD)
    previous = jnp.zeros((row_count, q_width), jnp.float32)
    decoded_list = []
    kept_list = []
    for step_idx in range(step_count):
        queries = (step_input[:, step_idx].astype(jnp.float32) + previous).astype(jnp.bfloat16)
        received = lax.all_to_all(to_slots(queries), "dp", split_axis=0, concat_axis=0, tiled=True)
        lead_shape = received.shape[:2]
        prompt_queries = received.reshape(-1, kv_heads, group_size, HD)
        scores = (
            jnp.einsum(
                "skgd,tkd->skgt", prompt_queries, pol_keys, preferred_element_type=jnp.float32
            )
            * inv_scale
        )
        prompt_weight, prompt_weight_sum, prompt_top_score = softmax_pieces(scores, prompt_valid)
        prompt_summed = jnp.einsum(
            "skgt,tkd->skgd",
            prompt_weight.astype(jnp.bfloat16),
            pol_values,
            preferred_element_type=jnp.float32,
        )
        part_out = (
            (prompt_summed / prompt_weight_sum[..., None])
            .astype(jnp.bfloat16)
            .reshape(lead_shape + (q_width,))
        )
        part_lse = (prompt_top_score + jnp.log(prompt_weight_sum)).reshape(lead_shape + (q_heads,))
        back_out = lax.all_to_all(part_out, "dp", split_axis=0, concat_axis=0, tiled=True)
        back_lse = lax.all_to_all(part_lse, "dp", split_axis=0, concat_axis=0, tiled=True)
        results = (back_out, back_lse, received)
        back_out = results[0]
        back_lse = results[1]
        kept_list.append(results[2])
        prompt_out = jnp.take(back_out.reshape(slot_count, q_width), slot_index, axis=0).astype(
            jnp.float32
        )
        prompt_lse = jnp.take(back_lse.reshape(slot_count, q_heads), slot_index, axis=0)
        query_heads = queries.reshape(row_count, kv_heads, group_size, HD)
        scores = (
            jnp.einsum(
                "rkgd,rtkd->rkgt", query_heads, resp_keys, preferred_element_type=jnp.float32
            )
            * inv_scale
        )
        reply_valid = jnp.where(
            reply_iota[None, :] < resp_slots,
            reply_iota[None, :] < resp_len[:, None],
            reply_iota[None, :] <= resp_slots + step_idx,
        )
        weight, weight_sum, top_score = softmax_pieces(scores, reply_valid[:, None, None, :])
        summed = jnp.einsum(
            "rkgt,rtkd->rkgd",
            weight.astype(jnp.bfloat16),
            resp_values,
            preferred_element_type=jnp.float32,
        )
        own_out = (summed / weight_sum[..., None]).reshape(row_count, q_heads, HD)
        own_lse = (top_score + jnp.log(weight_sum)).reshape(row_count, q_heads)
        joint_lse = jnp.maximum(prompt_lse, own_lse)
        prompt_wt = jnp.exp(prompt_lse - joint_lse)
        own_wt = jnp.exp(own_lse - joint_lse)
        blended = (
            prompt_wt[..., None] * prompt_out.reshape(row_count, q_heads, HD)
            + own_wt[..., None] * own_out
        ) / (prompt_wt + own_wt)[..., None]
        decoded_now = blended.reshape(row_count, q_width).astype(jnp.bfloat16)
        decoded_list.append(decoded_now)
        previous = lax.optimization_barrier(decoded_now).astype(jnp.float32)
    recv_kv, recv_live = (
        lax.all_to_all(to_slots(own_all), "dp", split_axis=0, concat_axis=0, tiled=True),
        lax.all_to_all(to_slots(live_len), "dp", split_axis=0, concat_axis=0, tiled=True),
    )
    recv_queries = jnp.stack(kept_list, axis=2)
    ref_keys = ref_prompt[0, :, 0].reshape(prompt_width, kv_heads, HD)
    ref_values = ref_prompt[0, :, 1].reshape(prompt_width, kv_heads, HD)
    slot_kv = recv_kv.reshape(slot_count, resp_slots + step_count, 2, kv_width)
    slot_keys = slot_kv[:, :, 0].reshape(slot_count, -1, kv_heads, HD)
    slot_values = slot_kv[:, :, 1].reshape(slot_count, -1, kv_heads, HD)
    slot_len = recv_live.reshape(slot_count).astype(jnp.int32)
    slot_queries = recv_queries.reshape(slot_count, step_count, q_width)
    probe_heads = probe.reshape(kv_heads, group_size, HD)
    prompt_mask = jnp.broadcast_to(prompt_valid[None, :], (slot_count, prompt_width))
    score_list = []
    for step_idx in range(step_count):
        queries = slot_queries[:, step_idx].reshape(slot_count, kv_heads, group_size, HD)
        prompt_scores = (
            jnp.einsum("skgd,tkd->skgt", queries, ref_keys, preferred_element_type=jnp.float32)
            * inv_scale
        )
        reply_scores = (
            jnp.einsum("skgd,stkd->skgt", queries, slot_keys, preferred_element_type=jnp.float32)
            * inv_scale
        )
        reply_valid = jnp.where(
            reply_iota[None, :] < resp_slots,
            reply_iota[None, :] < slot_len[:, None],
            reply_iota[None, :] <= resp_slots + step_idx,
        )
        key_valid = jnp.concatenate([prompt_mask, reply_valid], axis=1)
        weight, weight_sum, top_score = softmax_pieces(
            jnp.concatenate([prompt_scores, reply_scores], axis=-1), key_valid[:, None, None, :]
        )
        weight_low = weight.astype(jnp.bfloat16)
        summed = jnp.einsum(
            "skgt,tkd->skgd",
            weight_low[..., :prompt_width],
            ref_values,
            preferred_element_type=jnp.float32,
        )
        summed = summed + jnp.einsum(
            "skgt,stkd->skgd",
            weight_low[..., prompt_width:],
            slot_values,
            preferred_element_type=jnp.float32,
        )
        ref_out = summed / weight_sum[..., None]
        score_list.append(
            jnp.einsum("skgd,kgd->s", ref_out, probe_heads, precision=lax.Precision.HIGHEST)
        )
    head_terms = jnp.stack(score_list, axis=1)
    head_total = lax.psum(head_terms, "tensor")
    ref_score = jnp.where(slot_len[:, None] > 0, head_total, jnp.zeros((), jnp.float32)).reshape(
        1, slot_count, step_count
    )
    return (jnp.stack(decoded_list, axis=1), ref_score)


def ring_order(count):
    return list(range(0, count, 2)) + list(range(count - 1, 0, -2))


def iota(shape, dim):
    return lax.broadcasted_iota(jnp.int32, shape, dim)


def split_matrix(pairs):
    i = iota((2 * pairs, 2 * pairs), 0)
    j = iota((2 * pairs, 2 * pairs), 1)
    src = jnp.where(i < pairs, 2 * i, 2 * (i - pairs) + 1)
    return jnp.where(src == j, 1.0, 0.0).astype(jnp.bfloat16)


def swap_matrix(outer, inner):
    n = outer * inner
    i = iota((n, n), 0)
    j = iota((n, n), 1)
    src = (i % outer) * inner + i // outer
    return jnp.where(src == j, 1.0, 0.0).astype(jnp.bfloat16)


def mm(a, b):
    return jnp.dot(a, b, preferred_element_type=jnp.float32)


def mm_t(a, b):
    return lax.dot_general(a, b, (((1,), (1,)), ((), ())), preferred_element_type=jnp.float32)


def slots_kernel(owner_ref, len_ref, fin_ref, slot_ref, count_ref):
    peers = count_ref.shape[0]
    slots = slot_ref.shape[1]
    capacity = slots // peers
    for i in range(slots):
        slot_ref[0, i] = -1
        slot_ref[1, i] = 1
        slot_ref[2, i] = 0
    for o in range(peers):
        count_ref[o] = 0

    def place(r, c):
        o = jnp.clip(owner_ref[r], 0, peers - 1)
        k = count_ref[o]
        at = o * capacity + jnp.minimum(k, capacity - 1)
        slot_ref[0, at] = r
        slot_ref[1, at] = len_ref[r]
        slot_ref[2, at] = fin_ref[r]
        count_ref[o] = k + 1
        return c

    lax.fori_loop(0, owner_ref.shape[0], place, 0, unroll=4)


def slot_tables(row_owner, resp_len, finished, peers, capacity):
    smem = pl.BlockSpec(memory_space=pltpu.SMEM)
    return pl.pallas_call(
        slots_kernel,
        in_specs=[smem] * 3,
        out_specs=smem,
        out_shape=jax.ShapeDtypeStruct((3, peers * capacity), jnp.int32),
        scratch_shapes=[pltpu.SMEM((peers,), jnp.int32)],
        name="slots",
    )(row_owner, resp_len, finished)


def prep_kernel(slot_ref, x_hbm, rc_hbm, nk_hbm, xs_ref, ko_ref, vo_ref, xbuf, rcbuf, nkbuf, sem):
    peers, width, kv_width = ko_ref.shape
    _, capacity, old, _, _ = rcbuf.shape
    steps = nkbuf.shape[2]
    flights = []
    for o in range(peers):
        flight = []
        for k in range(capacity):
            row = jnp.maximum(slot_ref[0, o * capacity + k], 0)
            flight += [
                pltpu.make_async_copy(x_hbm.at[row], xbuf.at[o, k], sem.at[o, k, 0]),
                pltpu.make_async_copy(rc_hbm.at[row], rcbuf.at[o, k], sem.at[o, k, 1]),
                pltpu.make_async_copy(nk_hbm.at[row], nkbuf.at[o, k], sem.at[o, k, 2]),
            ]
        for c in flight:
            c.start()
        flights.append(flight)
    n_old, n_new = capacity * old, capacity * steps
    split_rc = split_matrix(n_old)
    split_nk = split_matrix(n_new)
    to_steps = swap_matrix(capacity, steps)
    zero = jnp.zeros((width - n_old - n_new, kv_width), jnp.float32)
    for o in range(peers):
        for c in flights[o]:
            c.wait()
        rc = mm(split_rc, rcbuf[o].reshape(2 * n_old, kv_width))
        nk = mm(split_nk, nkbuf[o].reshape(2 * n_new, kv_width))
        ko_ref[o] = jnp.concatenate([rc[:n_old], nk[:n_new], zero], 0).astype(jnp.bfloat16)
        vo_ref[o] = jnp.concatenate([rc[n_old:], nk[n_new:], zero], 0).astype(jnp.bfloat16)
        xs_ref[o] = mm(to_steps, xbuf[o].reshape(n_new, -1)).astype(jnp.bfloat16)


def prepare(slots, x, rc, nk, peers, capacity, width):
    _, steps, q_width = x.shape
    old = rc.shape[1]
    kv_width = rc.shape[3]
    smem = pl.BlockSpec(memory_space=pltpu.SMEM)
    vmem = pl.BlockSpec(memory_space=pltpu.VMEM)
    anyspec = pl.BlockSpec(memory_space=pl.ANY)
    bf = jnp.bfloat16
    return pl.pallas_call(
        prep_kernel,
        in_specs=[smem] + [anyspec] * 3,
        out_specs=[vmem] * 3,
        out_shape=[
            jax.ShapeDtypeStruct((peers, steps * capacity, q_width), bf),
            jax.ShapeDtypeStruct((peers, width, kv_width), bf),
            jax.ShapeDtypeStruct((peers, width, kv_width), bf),
        ],
        scratch_shapes=[
            pltpu.VMEM((peers, capacity, steps, q_width), bf),
            pltpu.VMEM((peers, capacity, old, 2, kv_width), bf),
            pltpu.VMEM((peers, capacity, steps, 2, kv_width), bf),
            pltpu.SemaphoreType.DMA((peers, capacity, 3)),
        ],
        compiler_params=pltpu.CompilerParams(vmem_limit_bytes=24 << 20),
        cost_estimate=pl.CostEstimate(flops=0, transcendentals=0, bytes_accessed=12 << 20),
        name="prep",
    )(slots, x, rc, nk)


def own_masks(slot_ref, base, rows, old, steps, width):
    lane = iota((rows, width), 1)
    sub = iota((rows, width), 0)
    split = rows * old
    is_old = lane < split
    key_row = jnp.where(is_old, lane // old, (lane - split) // steps)
    key_pos = jnp.where(is_old, lane % old, (lane - split) % steps)
    limit = jnp.zeros((rows, width), jnp.int32)
    for k in range(rows):
        limit = jnp.where(sub == k, slot_ref[1, base + k], limit)
    mine = (key_row == sub) & (lane < rows * (old + steps))
    return [
        mine & (key_pos < jnp.where(is_old, limit, step_idx + 1)) for step_idx in range(steps)
    ]


def make_work(pieces, begin, last, earlier, capacity, steps, old, kv_heads, group):
    head_rows = group * capacity
    inv_scale = 1.0 / math.sqrt(HD)
    first = begin == 0

    def body(*refs):
        refs = list(refs)
        me_ref, table_ref, plen_ref, slot_ref = refs[:4]
        xs_hbm, ko_hbm, vo_hbm, probe_ref = refs[4:8]
        refs = refs[8:]
        pols, refs = refs[:pieces], refs[pieces:]
        rfs, refs = refs[:pieces], refs[pieces:]
        if not first:
            refs = refs[1:]
        olds, refs = refs[:earlier], refs[earlier:]
        dec_hbm, score_ref = refs[:2]
        polbuf, refbuf, xs, kc, vp, vr, obuf, insem, outsem = refs[2:]
        width = kc.shape[1] // 3
        kv_width = kv_heads * HD
        me = me_ref[0]
        owners = [table_ref[me, begin + p] for p in range(pieces)]
        loads = []
        for p in range(pieces):
            o = owners[p]
            loads.append(
                [
                    pltpu.make_async_copy(pols[p].at[0], polbuf.at[p], insem.at[p, 0]),
                    pltpu.make_async_copy(rfs[p].at[0], refbuf.at[p], insem.at[p, 1]),
                    pltpu.make_async_copy(xs_hbm.at[o], xs.at[p], insem.at[p, 2]),
                    pltpu.make_async_copy(
                        ko_hbm.at[o], kc.at[p, pl.ds(width, width)], insem.at[p, 3]
                    ),
                    pltpu.make_async_copy(
                        vo_hbm.at[o], vr.at[p, pl.ds(width, width)], insem.at[p, 4]
                    ),
                ]
            )
        for load in loads:
            for c in load:
                c.start()
        split_p = split_matrix(width)
        to_rows = swap_matrix(steps, capacity)
        masks = [
            own_masks(slot_ref, owners[p] * capacity, capacity, old, steps, width)
            for p in range(pieces)
        ]
        lane = iota((head_rows, width), 1)
        pmask = [lane < plen_ref[0 if first else owners[p]] for p in range(pieces)]
        weights = [
            jnp.concatenate(
                [
                    jnp.broadcast_to(
                        probe_ref[g * group + h : g * group + h + 1, :], (capacity, HD)
                    )
                    for h in range(group)
                ],
                0,
            )
            for g in range(kv_heads)
        ]
        for p in range(pieces):
            for c in loads[p]:
                c.wait()
            both = mm(split_p, polbuf[p].reshape(2 * width, kv_width)).astype(jnp.bfloat16)
            kc[p, :width] = both[:width]
            vp[p] = both[width:]
            both = mm(split_p, refbuf[p].reshape(2 * width, kv_width)).astype(jnp.bfloat16)
            kc[p, 2 * width :] = both[:width]
            vr[p, :width] = both[width:]
        prev = [[None] * kv_heads for _ in range(pieces)]
        done = [[None] * steps for _ in range(pieces)]
        totals = [[None] * steps for _ in range(pieces)]
        for s in range(steps):
            for p in range(pieces):
                omask = jnp.concatenate([masks[p][s]] * group, 0)
                x = xs[p, s * capacity : (s + 1) * capacity, :].astype(jnp.float32)
                parts = []
                total = jnp.zeros((head_rows, HD), jnp.float32)
                for g in range(kv_heads):
                    at = slice(g * HD, (g + 1) * HD)
                    q = jnp.concatenate(
                        [x[:, (g * group + h) * HD : (g * group + h + 1) * HD] for h in range(group)],
                        0,
                    )
                    if s > 0:
                        q = q + prev[p][g]
                    q = q.astype(jnp.bfloat16)
                    z = mm_t(q, kc[p, :, at]) * inv_scale
                    zp = jnp.where(pmask[p], z[:, :width], -jnp.inf)
                    zo = jnp.where(omask, z[:, width : 2 * width], -jnp.inf)
                    zr = jnp.where(pmask[p], z[:, 2 * width :], -jnp.inf)
                    top_p = jnp.max(zp, axis=1, keepdims=True)
                    top_o = jnp.max(zo, axis=1, keepdims=True)
                    wp = jnp.exp(zp - top_p)
                    wo = jnp.exp(zo - top_o)
                    lp = jnp.sum(wp, axis=1, keepdims=True)
                    lo = jnp.sum(wo, axis=1, keepdims=True)
                    accp = mm(wp.astype(jnp.bfloat16), vp[p, :, at])
                    acco = mm(wo.astype(jnp.bfloat16), vr[p, width:, at])
                    out_p = (accp * (1.0 / lp)).astype(jnp.bfloat16).astype(jnp.float32)
                    top = jnp.maximum(top_p, top_o)
                    a = lp * jnp.exp(top_p - top)
                    c = jnp.exp(top_o - top)
                    inv = 1.0 / (a + lo * c)
                    mix = out_p * (a * inv) + acco * (c * inv)
                    mix = mix.astype(jnp.bfloat16).astype(jnp.float32)
                    prev[p][g] = mix
                    parts += [mix[h * capacity : (h + 1) * capacity] for h in range(group)]
                    top_r = jnp.maximum(jnp.max(zr, axis=1, keepdims=True), top_o)
                    wr = jnp.exp(zr - top_r)
                    wro = jnp.exp(zo - top_r)
                    lr = jnp.sum(wr + wro, axis=1, keepdims=True)
                    acc = mm(
                        jnp.concatenate([wr.astype(jnp.bfloat16), wro.astype(jnp.bfloat16)], 1),
                        vr[p, :, at],
                    )
                    total = total + (acc * (1.0 / lr)) * weights[g]
                done[p][s] = jnp.concatenate(parts, 1)
                fold = total[:capacity]
                for h in range(1, group):
                    fold = fold + total[h * capacity : (h + 1) * capacity]
                totals[p][s] = fold
        for p in range(pieces):
            d = jnp.concatenate(done[p], 0).astype(jnp.bfloat16)
            obuf[p] = mm(to_rows, d).astype(jnp.bfloat16).reshape(obuf.shape[1:])
            for k in range(capacity):
                row = slot_ref[0, owners[p] * capacity + k]

                @pl.when(row >= 0)
                def _():
                    pltpu.make_async_copy(obuf.at[p, k], dec_hbm.at[row], outsem.at[p, k]).start()

        out_lane = iota((capacity, HD), 1)
        out_sub = iota((capacity, HD), 0)
        for p in range(pieces):
            live = jnp.zeros((capacity, HD), jnp.int32)
            for k in range(capacity):
                live = jnp.where(out_sub == k, slot_ref[2, owners[p] * capacity + k], live)
            here = (out_lane == me * capacity + out_sub) & (live == 1)
            rows = []
            for s in range(steps):
                value = jnp.sum(totals[p][s], axis=1, keepdims=True)
                rows.append(jnp.sum(jnp.where(here, value, 0.0), axis=0, keepdims=True))
            rows = jnp.concatenate(rows, 0)
            if last:
                for t in range(score_ref.shape[1]):
                    score_ref[owners[p], t] = rows
            else:
                score_ref[p] = rows
        if last:
            n = 0
            for part in olds:
                for i in range(part.shape[0]):
                    for t in range(score_ref.shape[1]):
                        score_ref[table_ref[me, n], t] = part[i]
                    n += 1
        for p in range(pieces):
            for k in range(capacity):
                row = slot_ref[0, owners[p] * capacity + k]

                @pl.when(row >= 0)
                def _():
                    pltpu.make_async_copy(obuf.at[p, k], dec_hbm.at[row], outsem.at[p, k]).wait()

    return body


def work_pieces(me, table, plen, slots, prep, probe, pols, rfs, dec, olds, shape, begin, last, old, halves):
    pieces = len(pols)
    first = begin == 0
    xs, ko, vo = prep
    _, steps, q_width = shape
    peers, width, kv_width = ko.shape
    capacity = xs.shape[1] // steps
    kv_heads = kv_width // HD
    group = q_width // kv_width
    body = make_work(pieces, begin, last, len(olds), capacity, steps, old, kv_heads, group)
    smem = pl.BlockSpec(memory_space=pltpu.SMEM)
    vmem = pl.BlockSpec(memory_space=pltpu.VMEM)
    anyspec = pl.BlockSpec(memory_space=pl.ANY)
    args = [me, table, plen, slots, xs, ko, vo, probe, *pols, *rfs]
    specs = [smem] * 4 + [anyspec] * 3 + [vmem] + [anyspec] * (2 * pieces)
    alias = {}
    if not first:
        alias = {len(args): 0}
        args.append(dec)
        specs.append(anyspec)
    args += olds
    specs += [vmem] * len(olds)
    bf = jnp.bfloat16
    scores = (peers, halves, steps, HD) if last else (pieces, steps, HD)
    return pl.pallas_call(
        body,
        in_specs=specs,
        out_specs=[anyspec, vmem],
        out_shape=[
            jax.ShapeDtypeStruct(shape, bf),
            jax.ShapeDtypeStruct(scores, jnp.float32),
        ],
        scratch_shapes=[
            pltpu.VMEM((pieces, width, 2, kv_width), bf),
            pltpu.VMEM((pieces, width, 2, kv_width), bf),
            pltpu.VMEM((pieces, capacity * steps, q_width), bf),
            pltpu.VMEM((pieces, 3 * width, kv_width), bf),
            pltpu.VMEM((pieces, width, kv_width), bf),
            pltpu.VMEM((pieces, 2 * width, kv_width), bf),
            pltpu.VMEM((pieces, capacity, steps, q_width), bf),
            pltpu.SemaphoreType.DMA((pieces, 5)),
            pltpu.SemaphoreType.DMA((pieces, capacity)),
        ],
        input_output_aliases=alias,
        compiler_params=pltpu.CompilerParams(vmem_limit_bytes=24 << 20),
        cost_estimate=pl.CostEstimate(flops=0, transcendentals=0, bytes_accessed=16 << 20),
        name="work",
    )(*args)


def ring_fits(step_input, new_kv, resp_cache, policy_prompt, *rest):
    peers = lax.axis_size("dp")
    row_count, step_count, q_width = step_input.shape
    old = resp_cache.shape[1]
    kv_width = new_kv.shape[3]
    width = policy_prompt.shape[1]
    capacity = max(2, (row_count + peers - 1) // peers)
    gathered = 2 * peers * policy_prompt.size
    exchanged = 2 * step_input.size + new_kv.size + resp_cache.size
    return (
        gathered <= exchanged
        and peers % 2 == 0
        and peers >= 4
        and capacity % 8 == 0
        and peers * capacity <= HD
        and capacity * (old + step_count) <= width
        and width % HD == 0
        and q_width % kv_width == 0
    )


def per_device_ring(
    step_input,
    new_kv,
    resp_cache,
    policy_prompt,
    ref_prompt,
    prompt_len,
    resp_len,
    row_owner,
    finished,
    probe,
):
    row_count, step_count, q_width = step_input.shape
    peers = lax.axis_size("dp")
    halves = lax.axis_size("tensor")
    width = policy_prompt.shape[1]
    capacity = max(2, (row_count + peers - 1) // peers)
    old = resp_cache.shape[1]
    ring = ring_order(peers)
    forward = [(ring[i], ring[(i + 1) % peers]) for i in range(peers)]
    backward = [(b, a) for a, b in forward]
    spot = {d: i for i, d in enumerate(ring)}
    offsets = [0]
    for d in range(1, peers // 2):
        offsets += [-d, d]
    offsets.append(peers // 2)
    table = [[ring[(spot[dev] + off) % peers] for off in offsets] for dev in range(peers)]
    table = jnp.array(table, jnp.int32)
    me = lax.axis_index("dp").astype(jnp.int32).reshape(1)
    probe_heads = probe.reshape(q_width // HD, HD)

    def hop(value, pairs):
        return lax.ppermute(value, "dp", pairs)

    pf = hop(policy_prompt, forward)
    pb = hop(policy_prompt, backward)
    rf = hop(ref_prompt, forward)
    rb = hop(ref_prompt, backward)
    plen_all = lax.all_to_all(
        jnp.broadcast_to(prompt_len, (peers,)), "dp", split_axis=0, concat_axis=0, tiled=True
    )
    slots = slot_tables(row_owner, resp_len, finished, peers, capacity)
    prep = prepare(slots, step_input, resp_cache, new_kv, peers, capacity, width)

    def work(pols, rfs, dec, olds, begin, last=False):
        plen = prompt_len if begin == 0 else plen_all
        return work_pieces(
            me, table, plen, slots, prep, probe_heads, pols, rfs, dec, olds,
            step_input.shape, begin, last, old, halves,
        )

    dec, score = work([policy_prompt], [ref_prompt], None, [], 0)
    scores = [score]
    begin = 1
    for d in range(1, peers // 2):
        now = [pf, pb], [rf, rb]
        pf = hop(pf, forward)
        if d + 1 < peers // 2:
            pb = hop(pb, backward)
            rf = hop(rf, forward)
        rb = hop(rb, backward)
        dec, score = work(*now, dec, [], begin)
        scores.append(score)
        begin += 2
    dec, send = work([pf], [rb], dec, scores, begin, True)
    got = lax.all_to_all(
        send.reshape(peers * halves, step_count, HD),
        ("dp", "tensor"),
        split_axis=0,
        concat_axis=0,
        tiled=True,
    )
    total = jnp.sum(got, axis=0)[:, : peers * capacity]
    return dec, total.T.reshape(1, peers * capacity, step_count)


def solution(mesh):
    in_specs = (
        P(("groups", "dp"), None, "tensor"),
        P(("groups", "dp"), None, None, "tensor"),
        P(("groups", "dp"), None, None, "tensor"),
        P(("groups", "dp"), None, None, "tensor"),
        P(("groups", "dp"), None, None, "tensor"),
        P(("groups", "dp")),
        P(("groups", "dp")),
        P(("groups", "dp")),
        P(("groups", "dp")),
        P("tensor"),
    )
    out_specs = (P(("groups", "dp"), None, "tensor"), P(("groups", "dp"), None, None))

    def run(*args):
        return per_device_ring(*args) if ring_fits(*args) else per_device(*args)

    return jax.shard_map(
        run, mesh=mesh, in_specs=in_specs, out_specs=out_specs, check_vma=False
    )
```

```python
import math

import jax
import jax.numpy as jnp
from jax import lax
from jax.experimental import pallas as pl
from jax.experimental.pallas import tpu as pltpu
from jax.sharding import PartitionSpec as P

HD = 128


def softmax_pieces(scores, key_valid):
    masked = jnp.where(key_valid, scores, -jnp.inf)
    top_score = jnp.max(masked, axis=-1, keepdims=True)
    weight = jnp.exp(masked - top_score)
    return (weight, jnp.sum(weight, axis=-1), top_score[..., 0])


def per_device(
    step_input,
    new_kv,
    resp_cache,
    policy_prompt,
    ref_prompt,
    prompt_len,
    resp_len,
    row_owner,
    finished,
    probe,
):
    row_count = step_input.shape[0]
    step_count = step_input.shape[1]
    q_width = step_input.shape[2]
    kv_width = new_kv.shape[3]
    q_heads = q_width // HD
    kv_heads = kv_width // HD
    group_size = q_heads // kv_heads
    inv_scale = 1.0 / math.sqrt(HD)
    peer_count = lax.axis_size("dp")
    capacity = max(2, (row_count + peer_count - 1) // peer_count)
    slot_count = peer_count * capacity
    resp_slots = resp_cache.shape[1]
    prompt_width = policy_prompt.shape[1]
    row_iota = jnp.arange(row_count, dtype=jnp.int32)
    same_owner = (row_owner[:, None] == row_owner[None, :]) & (
        row_iota[None, :] < row_iota[:, None]
    )
    slot_index = row_owner * capacity + jnp.sum(same_owner.astype(jnp.int32), axis=1)
    dispatch = slot_index[:, None] == jnp.arange(slot_count, dtype=jnp.int32)[None, :]
    slot_used = jnp.any(dispatch, axis=0)
    slot_row = jnp.sum(jnp.where(dispatch, row_iota[:, None], 0), axis=0)

    def to_slots(rows_data):
        picked = jnp.take(rows_data, slot_row, axis=0)
        mask_shape = (slot_count,) + (1,) * (rows_data.ndim - 1)
        picked = jnp.where(slot_used.reshape(mask_shape), picked, jnp.zeros_like(picked))
        return picked.reshape((peer_count, capacity) + rows_data.shape[1:])

    live_len = jnp.where(finished == 1, resp_len, 0).astype(jnp.bfloat16)
    own_all = jnp.concatenate([resp_cache, new_kv], axis=1)
    reply_iota = jnp.arange(resp_slots + step_count)
    pol_keys = policy_prompt[0, :, 0].reshape(prompt_width, kv_heads, HD)
    pol_values = policy_prompt[0, :, 1].reshape(prompt_width, kv_heads, HD)
    prompt_valid = jnp.arange(prompt_width) < prompt_len[0]
    resp_keys = own_all[:, :, 0].reshape(row_count, -1, kv_heads, HD)
    resp_values = own_all[:, :, 1].reshape(row_count, -1, kv_heads, HD)
    previous = jnp.zeros((row_count, q_width), jnp.float32)
    decoded_list = []
    query_list = []
    kept_list = []
    for step_idx in range(step_count):
        queries = (step_input[:, step_idx].astype(jnp.float32) + previous).astype(jnp.bfloat16)
        query_list.append(queries)
        received = lax.all_to_all(to_slots(queries), "dp", split_axis=0, concat_axis=0, tiled=True)
        lead_shape = received.shape[:2]
        prompt_queries = received.reshape(-1, kv_heads, group_size, HD)
        scores = (
            jnp.einsum(
                "skgd,tkd->skgt", prompt_queries, pol_keys, preferred_element_type=jnp.float32
            )
            * inv_scale
        )
        prompt_weight, prompt_weight_sum, prompt_top_score = softmax_pieces(scores, prompt_valid)
        prompt_summed = jnp.einsum(
            "skgt,tkd->skgd",
            prompt_weight.astype(jnp.bfloat16),
            pol_values,
            preferred_element_type=jnp.float32,
        )
        part_out = (
            (prompt_summed / prompt_weight_sum[..., None])
            .astype(jnp.bfloat16)
            .reshape(lead_shape + (q_width,))
        )
        part_lse = (prompt_top_score + jnp.log(prompt_weight_sum)).reshape(lead_shape + (q_heads,))
        back_out = lax.all_to_all(part_out, "dp", split_axis=0, concat_axis=0, tiled=True)
        back_lse = lax.all_to_all(part_lse, "dp", split_axis=0, concat_axis=0, tiled=True)
        results = (back_out, back_lse, received)
        back_out = results[0]
        back_lse = results[1]
        kept_list.append(results[2])
        prompt_out = jnp.take(back_out.reshape(slot_count, q_width), slot_index, axis=0).astype(
            jnp.float32
        )
        prompt_lse = jnp.take(back_lse.reshape(slot_count, q_heads), slot_index, axis=0)
        query_heads = queries.reshape(row_count, kv_heads, group_size, HD)
        scores = (
            jnp.einsum(
                "rkgd,rtkd->rkgt", query_heads, resp_keys, preferred_element_type=jnp.float32
            )
            * inv_scale
        )
        reply_valid = jnp.where(
            reply_iota[None, :] < resp_slots,
            reply_iota[None, :] < resp_len[:, None],
            reply_iota[None, :] <= resp_slots + step_idx,
        )
        weight, weight_sum, top_score = softmax_pieces(scores, reply_valid[:, None, None, :])
        summed = jnp.einsum(
            "rkgt,rtkd->rkgd",
            weight.astype(jnp.bfloat16),
            resp_values,
            preferred_element_type=jnp.float32,
        )
        own_out = (summed / weight_sum[..., None]).reshape(row_count, q_heads, HD)
        own_lse = (top_score + jnp.log(weight_sum)).reshape(row_count, q_heads)
        joint_lse = jnp.maximum(prompt_lse, own_lse)
        prompt_wt = jnp.exp(prompt_lse - joint_lse)
        own_wt = jnp.exp(own_lse - joint_lse)
        blended = (
            prompt_wt[..., None] * prompt_out.reshape(row_count, q_heads, HD)
            + own_wt[..., None] * own_out
        ) / (prompt_wt + own_wt)[..., None]
        decoded_now = blended.reshape(row_count, q_width).astype(jnp.bfloat16)
        decoded_list.append(decoded_now)
        previous = lax.optimization_barrier(decoded_now).astype(jnp.float32)
    recv_kv, recv_live = (
        lax.all_to_all(to_slots(own_all), "dp", split_axis=0, concat_axis=0, tiled=True),
        lax.all_to_all(to_slots(live_len), "dp", split_axis=0, concat_axis=0, tiled=True),
    )
    recv_queries = jnp.stack(kept_list, axis=2)
    ref_keys = ref_prompt[0, :, 0].reshape(prompt_width, kv_heads, HD)
    ref_values = ref_prompt[0, :, 1].reshape(prompt_width, kv_heads, HD)
    slot_kv = recv_kv.reshape(slot_count, resp_slots + step_count, 2, kv_width)
    slot_keys = slot_kv[:, :, 0].reshape(slot_count, -1, kv_heads, HD)
    slot_values = slot_kv[:, :, 1].reshape(slot_count, -1, kv_heads, HD)
    slot_len = recv_live.reshape(slot_count).astype(jnp.int32)
    slot_queries = recv_queries.reshape(slot_count, step_count, q_width)
    probe_heads = probe.reshape(kv_heads, group_size, HD)
    prompt_mask = jnp.broadcast_to(prompt_valid[None, :], (slot_count, prompt_width))
    score_list = []
    for step_idx in range(step_count):
        queries = slot_queries[:, step_idx].reshape(slot_count, kv_heads, group_size, HD)
        prompt_scores = (
            jnp.einsum("skgd,tkd->skgt", queries, ref_keys, preferred_element_type=jnp.float32)
            * inv_scale
        )
        reply_scores = (
            jnp.einsum("skgd,stkd->skgt", queries, slot_keys, preferred_element_type=jnp.float32)
            * inv_scale
        )
        reply_valid = jnp.where(
            reply_iota[None, :] < resp_slots,
            reply_iota[None, :] < slot_len[:, None],
            reply_iota[None, :] <= resp_slots + step_idx,
        )
        key_valid = jnp.concatenate([prompt_mask, reply_valid], axis=1)
        weight, weight_sum, top_score = softmax_pieces(
            jnp.concatenate([prompt_scores, reply_scores], axis=-1), key_valid[:, None, None, :]
        )
        weight_low = weight.astype(jnp.bfloat16)
        summed = jnp.einsum(
            "skgt,tkd->skgd",
            weight_low[..., :prompt_width],
            ref_values,
            preferred_element_type=jnp.float32,
        )
        summed = summed + jnp.einsum(
            "skgt,stkd->skgd",
            weight_low[..., prompt_width:],
            slot_values,
            preferred_element_type=jnp.float32,
        )
        ref_out = summed / weight_sum[..., None]
        score_list.append(
            jnp.einsum("skgd,kgd->s", ref_out, probe_heads, precision=lax.Precision.HIGHEST)
        )
    head_terms = jnp.stack(score_list, axis=1)
    head_total = lax.psum(head_terms, "tensor")
    ref_score = jnp.where(slot_len[:, None] > 0, head_total, jnp.zeros((), jnp.float32)).reshape(
        1, slot_count, step_count
    )
    return (jnp.stack(decoded_list, axis=1), ref_score)


def ring_order(count):
    return list(range(0, count, 2)) + list(range(count - 1, 0, -2))


def ring_owner(me, nth, count):
    half = lax.div(me, 2)
    spot = jnp.where(lax.rem(me, 2) == 0, half, count - 1 - half)
    step = (nth + 1) // 2
    spot = lax.rem(spot + (step if nth % 2 == 0 else count - step), count)
    return jnp.where(spot < count // 2, 2 * spot, 2 * (count - 1 - spot) + 1)


def iota(shape, dim):
    return lax.broadcasted_iota(jnp.int32, shape, dim)


def split_matrix(pairs):
    i = iota((2 * pairs, 2 * pairs), 0)
    j = iota((2 * pairs, 2 * pairs), 1)
    src = jnp.where(i < pairs, 2 * i, 2 * (i - pairs) + 1)
    return jnp.where(src == j, 1.0, 0.0).astype(jnp.bfloat16)


def swap_matrix(outer, inner):
    n = outer * inner
    i = iota((n, n), 0)
    j = iota((n, n), 1)
    src = (i % outer) * inner + i // outer
    return jnp.where(src == j, 1.0, 0.0).astype(jnp.bfloat16)


def mm(a, b):
    return jnp.dot(a, b, preferred_element_type=jnp.float32)


def mm_t(a, b):
    return lax.dot_general(a, b, (((1,), (1,)), ((), ())), preferred_element_type=jnp.float32)


def slots_kernel(owner_ref, len_ref, fin_ref, slot_ref, count_ref):
    peers = count_ref.shape[0]
    slots = slot_ref.shape[1]
    capacity = slots // peers
    for i in range(slots):
        slot_ref[0, i] = -1
        slot_ref[1, i] = 1
        slot_ref[2, i] = 0
    for o in range(peers):
        count_ref[o] = 0

    def place(r, c):
        o = jnp.clip(owner_ref[r], 0, peers - 1)
        k = count_ref[o]
        at = o * capacity + jnp.minimum(k, capacity - 1)
        slot_ref[0, at] = r
        slot_ref[1, at] = len_ref[r]
        slot_ref[2, at] = fin_ref[r]
        count_ref[o] = k + 1
        return c

    lax.fori_loop(0, owner_ref.shape[0], place, 0, unroll=4)


def slot_tables(row_owner, resp_len, finished, peers, capacity):
    smem = pl.BlockSpec(memory_space=pltpu.SMEM)
    return pl.pallas_call(
        slots_kernel,
        in_specs=[smem] * 3,
        out_specs=smem,
        out_shape=jax.ShapeDtypeStruct((3, peers * capacity), jnp.int32),
        scratch_shapes=[pltpu.SMEM((peers,), jnp.int32)],
        name="slots",
    )(row_owner, resp_len, finished)


def own_masks(slot_ref, base, rows, old, steps, width):
    lane = iota((rows, width), 1)
    sub = iota((rows, width), 0)
    split = rows * old
    is_old = lane < split
    key_row = jnp.where(is_old, lane // old, (lane - split) // steps)
    key_pos = jnp.where(is_old, lane % old, (lane - split) % steps)
    limit = jnp.zeros((rows, width), jnp.int32)
    for k in range(rows):
        limit = jnp.where(sub == k, slot_ref[1, base + k], limit)
    mine = (key_row == sub) & (lane < rows * (old + steps))
    return [
        mine & (key_pos < jnp.where(is_old, limit, step_idx + 1)) for step_idx in range(steps)
    ]


def make_work(peers, pieces, begin, last, earlier, capacity, steps, old, kv_heads, group):
    head_rows = group * capacity
    inv_scale = 1.0 / math.sqrt(HD)
    n_old, n_new = capacity * old, capacity * steps

    def body(*refs):
        refs = list(refs)
        me_ref, slot_ref = refs[:2]
        x_hbm, rc_hbm, nk_hbm, probe_ref = refs[2:6]
        refs = refs[6:]
        pols, refs = refs[:pieces], refs[pieces:]
        rfs, refs = refs[:pieces], refs[pieces:]
        if begin > 0:
            refs = refs[1:]
        olds, refs = refs[:earlier], refs[earlier:]
        dec_hbm, score_ref = refs[:2]
        polbuf, refbuf, xbuf, rcbuf, nkbuf, xs, kc, vc, qs, obuf, insem, rowsem, outsem = refs[2:]
        width = kc.shape[1] // 3
        kv_width = kv_heads * HD
        me = me_ref[0]
        owners = [ring_owner(me, begin + p, peers) for p in range(pieces)]
        loads, flights = [], []
        for p in range(pieces):
            flight = []
            for k in range(capacity):
                row = jnp.maximum(slot_ref[0, owners[p] * capacity + k], 0)
                flight += [
                    pltpu.make_async_copy(x_hbm.at[row], xbuf.at[p, k], rowsem.at[p, k, 0]),
                    pltpu.make_async_copy(rc_hbm.at[row], rcbuf.at[p, k], rowsem.at[p, k, 1]),
                    pltpu.make_async_copy(nk_hbm.at[row], nkbuf.at[p, k], rowsem.at[p, k, 2]),
                ]
            flights.append(flight)
            loads.append(
                [
                    pltpu.make_async_copy(pols[p].at[0], polbuf.at[p], insem.at[p, 0]),
                    pltpu.make_async_copy(rfs[p].at[0], refbuf.at[p], insem.at[p, 1]),
                ]
            )
        for p in range(pieces):
            for c in flights[p] + loads[p]:
                c.start()
        split_p = split_matrix(width)
        split_rc = split_matrix(n_old)
        split_nk = split_matrix(n_new)
        to_steps = swap_matrix(capacity, steps)
        to_rows = swap_matrix(steps, capacity)
        masks = [
            own_masks(slot_ref, owners[p] * capacity, capacity, old, steps, width)
            for p in range(pieces)
        ]
        lane = iota((capacity, width), 1).astype(jnp.float32)
        zero = jnp.zeros((width - n_old - n_new, kv_width), jnp.float32)
        pmask = []
        for p in range(pieces):
            for c in flights[p]:
                c.wait()
            rc = mm(split_rc, rcbuf[p].reshape(2 * n_old, kv_width))
            nk = mm(split_nk, nkbuf[p].reshape(2 * n_new, kv_width))
            own_k = jnp.concatenate([rc[:n_old], nk[:n_new], zero], 0).astype(jnp.bfloat16)
            own_v = jnp.concatenate([rc[n_old:], nk[n_new:], zero], 0).astype(jnp.bfloat16)
            kc[p, width : 2 * width] = own_k
            vc[p, width : 2 * width] = own_v
            xs[p] = mm(to_steps, xbuf[p].reshape(n_new, -1))
            for c in loads[p]:
                c.wait()
            both = mm(split_p, polbuf[p].reshape(2 * width, kv_width)).astype(jnp.bfloat16)
            kc[p, :width] = both[:width]
            vc[p, :width] = both[width:]
            both = mm(split_p, refbuf[p, :width].reshape(2 * width, kv_width)).astype(jnp.bfloat16)
            kc[p, 2 * width :] = both[:width]
            vc[p, 2 * width :] = both[width:]
            length = refbuf[p, width].astype(jnp.float32)[:1, :width]
            pmask.append(jnp.concatenate([lane < length] * group, 0))
        prev = [[None] * kv_heads for _ in range(pieces)]
        done = [[None] * steps for _ in range(pieces)]
        for s in range(steps):
            for p in range(pieces):
                omask = jnp.concatenate([masks[p][s]] * group, 0)
                parts = []
                for g in range(kv_heads):
                    at = slice(g * HD, (g + 1) * HD)
                    q = jnp.concatenate(
                        [
                            xs[p, s * capacity : (s + 1) * capacity, (g * group + h) * HD : (g * group + h + 1) * HD]
                            for h in range(group)
                        ],
                        0,
                    )
                    if s > 0:
                        q = q + prev[p][g]
                    q = q.astype(jnp.bfloat16)
                    qs[p, g, s * head_rows : (s + 1) * head_rows] = q
                    z = mm_t(q, kc[p, : 2 * width, at]) * inv_scale
                    zp = jnp.where(pmask[p], z[:, :width], -jnp.inf)
                    zo = jnp.where(omask, z[:, width:], -jnp.inf)
                    top_p = jnp.max(zp, axis=1, keepdims=True)
                    top_o = jnp.max(zo, axis=1, keepdims=True)
                    wp = jnp.exp(zp - top_p)
                    wo = jnp.exp(zo - top_o)
                    lp = jnp.sum(wp, axis=1, keepdims=True)
                    lo = jnp.sum(wo, axis=1, keepdims=True)
                    accp = mm(wp.astype(jnp.bfloat16), vc[p, :width, at])
                    acco = mm(wo.astype(jnp.bfloat16), vc[p, width : 2 * width, at])
                    out_p = (accp * (1.0 / lp)).astype(jnp.bfloat16).astype(jnp.float32)
                    top = jnp.maximum(top_p, top_o)
                    a = lp * jnp.exp(top_p - top)
                    c = jnp.exp(top_o - top)
                    inv = 1.0 / (a + lo * c)
                    mix = out_p * (a * inv) + acco * (c * inv)
                    mix = mix.astype(jnp.bfloat16).astype(jnp.float32)
                    prev[p][g] = mix
                    parts += [mix[h * capacity : (h + 1) * capacity] for h in range(group)]
                done[p][s] = jnp.concatenate(parts, 1)
        for p in range(pieces):
            d = jnp.concatenate(done[p], 0).astype(jnp.bfloat16)
            obuf[p] = mm(to_rows, d).astype(jnp.bfloat16).reshape(obuf.shape[1:])
            for k in range(capacity):
                row = slot_ref[0, owners[p] * capacity + k]

                @pl.when(row >= 0)
                def _():
                    pltpu.make_async_copy(obuf.at[p, k], dec_hbm.at[row], outsem.at[p, k]).start()

        out_lane = iota((capacity, HD), 1)
        out_sub = iota((capacity, HD), 0)
        for p in range(pieces):
            full = jnp.concatenate(
                [
                    jnp.concatenate([jnp.concatenate([masks[p][s]] * group, 0), pmask[p]], 1)
                    for s in range(steps)
                ],
                0,
            )
            total = [jnp.zeros((capacity, HD), jnp.float32) for _ in range(steps)]
            for g in range(kv_heads):
                at = slice(g * HD, (g + 1) * HD)
                z = mm_t(qs[p, g], kc[p, width:, at]) * inv_scale
                z = jnp.where(full, z, -jnp.inf)
                w = jnp.exp(z - jnp.max(z, axis=1, keepdims=True))
                acc = mm(w.astype(jnp.bfloat16), vc[p, width:, at])
                acc = acc * (1.0 / jnp.sum(w, axis=1, keepdims=True))
                for s in range(steps):
                    for h in range(group):
                        lo = (s * group + h) * capacity
                        weight = probe_ref[g * group + h : g * group + h + 1, :]
                        total[s] = total[s] + acc[lo : lo + capacity] * weight
            live = jnp.zeros((capacity, HD), jnp.int32)
            for k in range(capacity):
                live = jnp.where(out_sub == k, slot_ref[2, owners[p] * capacity + k], live)
            here = (out_lane == me * capacity + out_sub) & (live == 1)
            rows = []
            for s in range(steps):
                value = jnp.sum(total[s], axis=1, keepdims=True)
                rows.append(jnp.sum(jnp.where(here, value, 0.0), axis=0, keepdims=True))
            rows = jnp.concatenate(rows, 0)
            if last:
                for t in range(score_ref.shape[1]):
                    score_ref[owners[p], t] = rows
            else:
                score_ref[p] = rows
        if last:
            n = 0
            for part in olds:
                for i in range(part.shape[0]):
                    for t in range(score_ref.shape[1]):
                        score_ref[ring_owner(me, n, peers), t] = part[i]
                    n += 1
        for p in range(pieces):
            for k in range(capacity):
                row = slot_ref[0, owners[p] * capacity + k]

                @pl.when(row >= 0)
                def _():
                    pltpu.make_async_copy(obuf.at[p, k], dec_hbm.at[row], outsem.at[p, k]).wait()

    return body


def work_pieces(me, peers, slots, rows, probe, pols, rfs, dec, olds, begin, last, halves):
    x, rc, nk = rows
    pieces = len(pols)
    _, steps, q_width = x.shape
    _, width, _, kv_width = pols[0].shape
    old = rc.shape[1]
    capacity = slots.shape[1] // peers
    kv_heads = kv_width // HD
    group = q_width // kv_width
    body = make_work(peers, pieces, begin, last, len(olds), capacity, steps, old, kv_heads, group)
    smem = pl.BlockSpec(memory_space=pltpu.SMEM)
    vmem = pl.BlockSpec(memory_space=pltpu.VMEM)
    anyspec = pl.BlockSpec(memory_space=pltpu.HBM)
    x, rc, nk = (pltpu.with_memory_space_constraint(v, pltpu.HBM) for v in rows)
    args = [me, slots, x, rc, nk, probe, *pols, *rfs]
    specs = [smem] * 2 + [anyspec] * 3 + [vmem] + [anyspec] * (2 * pieces)
    alias = {}
    if begin > 0:
        alias = {len(args): 0}
        args.append(dec)
        specs.append(anyspec)
    args += olds
    specs += [vmem] * len(olds)
    bf = jnp.bfloat16
    scores = (peers, halves, steps, HD) if last else (pieces, steps, HD)
    return pl.pallas_call(
        body,
        in_specs=specs,
        out_specs=[anyspec, vmem],
        out_shape=[
            jax.ShapeDtypeStruct(x.shape, bf),
            jax.ShapeDtypeStruct(scores, jnp.float32),
        ],
        scratch_shapes=[
            pltpu.VMEM((pieces, width, 2, kv_width), bf),
            pltpu.VMEM((pieces, width + 1, 2, kv_width), bf),
            pltpu.VMEM((pieces, capacity, steps, q_width), bf),
            pltpu.VMEM((pieces, capacity, old, 2, kv_width), bf),
            pltpu.VMEM((pieces, capacity, steps, 2, kv_width), bf),
            pltpu.VMEM((pieces, capacity * steps, q_width), jnp.float32),
            pltpu.VMEM((pieces, 3 * width, kv_width), bf),
            pltpu.VMEM((pieces, 3 * width, kv_width), bf),
            pltpu.VMEM((pieces, kv_heads, steps * group * capacity, HD), bf),
            pltpu.VMEM((pieces, capacity, steps, q_width), bf),
            pltpu.SemaphoreType.DMA((pieces, 2)),
            pltpu.SemaphoreType.DMA((pieces, capacity, 3)),
            pltpu.SemaphoreType.DMA((pieces, capacity)),
        ],
        input_output_aliases=alias,
        compiler_params=pltpu.CompilerParams(vmem_limit_bytes=24 << 20),
        cost_estimate=pl.CostEstimate(flops=0, transcendentals=0, bytes_accessed=16 << 20),
        name="work",
    )(*args)


def ring_fits(step_input, new_kv, resp_cache, policy_prompt, *rest):
    peers = lax.axis_size("dp")
    row_count, step_count, q_width = step_input.shape
    old = resp_cache.shape[1]
    kv_width = new_kv.shape[3]
    width = policy_prompt.shape[1]
    capacity = max(2, (row_count + peers - 1) // peers)
    gathered = 2 * peers * policy_prompt.size
    exchanged = 2 * step_input.size + new_kv.size + resp_cache.size
    return (
        gathered <= exchanged
        and peers % 2 == 0
        and peers >= 4
        and capacity % 8 == 0
        and peers * capacity <= HD
        and capacity * (old + step_count) <= width
        and width % HD == 0
        and q_width % kv_width == 0
    )


def per_device_ring(
    step_input,
    new_kv,
    resp_cache,
    policy_prompt,
    ref_prompt,
    prompt_len,
    resp_len,
    row_owner,
    finished,
    probe,
):
    row_count, step_count, q_width = step_input.shape
    peers = lax.axis_size("dp")
    halves = lax.axis_size("tensor")
    capacity = max(2, (row_count + peers - 1) // peers)
    ring = ring_order(peers)
    forward = [(ring[i], ring[(i + 1) % peers]) for i in range(peers)]
    backward = [(b, a) for a, b in forward]
    me = lax.axis_index("dp").astype(jnp.int32).reshape(1)
    probe_heads = probe.reshape(q_width // HD, HD)

    def hop(value, pairs):
        return lax.ppermute(value, "dp", pairs)

    pf = hop(policy_prompt, forward)
    pb = hop(policy_prompt, backward)
    mark = jnp.broadcast_to(prompt_len.astype(jnp.bfloat16), (1, 1) + ref_prompt.shape[2:])
    ref0 = jnp.concatenate([ref_prompt, mark], axis=1)
    rf = hop(ref0, forward)
    rb = hop(ref0, backward)
    slots = slot_tables(row_owner, resp_len, finished, peers, capacity)
    rows = (step_input, resp_cache, new_kv)

    def work(pols, rfs, dec, olds, begin, last=False):
        return work_pieces(
            me, peers, slots, rows, probe_heads, pols, rfs, dec, olds, begin, last, halves
        )

    dec, score = work([policy_prompt], [ref0], None, [], 0)
    scores = [score]
    begin = 1
    for d in range(1, peers // 2):
        now = [pf, pb], [rf, rb]
        pf = hop(pf, forward)
        if d + 1 < peers // 2:
            pb = hop(pb, backward)
            rf = hop(rf, forward)
        rb = hop(rb, backward)
        dec, score = work(*now, dec, [], begin)
        scores.append(score)
        begin += len(now[0])
    dec, send = work([pf], [rb], dec, scores, begin, True)
    got = lax.all_to_all(
        send.reshape(peers * halves, step_count, HD),
        ("dp", "tensor"),
        split_axis=0,
        concat_axis=0,
        tiled=True,
    )
    total = jnp.sum(got, axis=0)[:, : peers * capacity]
    return dec, total.T.reshape(1, peers * capacity, step_count)


def solution(mesh):
    in_specs = (
        P(("groups", "dp"), None, "tensor"),
        P(("groups", "dp"), None, None, "tensor"),
        P(("groups", "dp"), None, None, "tensor"),
        P(("groups", "dp"), None, None, "tensor"),
        P(("groups", "dp"), None, None, "tensor"),
        P(("groups", "dp")),
        P(("groups", "dp")),
        P(("groups", "dp")),
        P(("groups", "dp")),
        P("tensor"),
    )
    out_specs = (P(("groups", "dp"), None, "tensor"), P(("groups", "dp"), None, None))

    def run(*args):
        return per_device_ring(*args) if ring_fits(*args) else per_device(*args)

    return jax.shard_map(
        run, mesh=mesh, in_specs=in_specs, out_specs=out_specs, check_vma=False
    )
```

```python
import math

import jax
import jax.numpy as jnp
from jax import lax
from jax.experimental import pallas as pl
from jax.experimental.pallas import tpu as pltpu
from jax.sharding import PartitionSpec as P

HD = 128


def softmax_pieces(scores, key_valid):
    masked = jnp.where(key_valid, scores, -jnp.inf)
    top_score = jnp.max(masked, axis=-1, keepdims=True)
    weight = jnp.exp(masked - top_score)
    return (weight, jnp.sum(weight, axis=-1), top_score[..., 0])


def per_device(
    step_input,
    new_kv,
    resp_cache,
    policy_prompt,
    ref_prompt,
    prompt_len,
    resp_len,
    row_owner,
    finished,
    probe,
):
    row_count = step_input.shape[0]
    step_count = step_input.shape[1]
    q_width = step_input.shape[2]
    kv_width = new_kv.shape[3]
    q_heads = q_width // HD
    kv_heads = kv_width // HD
    group_size = q_heads // kv_heads
    inv_scale = 1.0 / math.sqrt(HD)
    peer_count = lax.axis_size("dp")
    capacity = max(2, (row_count + peer_count - 1) // peer_count)
    slot_count = peer_count * capacity
    resp_slots = resp_cache.shape[1]
    prompt_width = policy_prompt.shape[1]
    row_iota = jnp.arange(row_count, dtype=jnp.int32)
    same_owner = (row_owner[:, None] == row_owner[None, :]) & (
        row_iota[None, :] < row_iota[:, None]
    )
    slot_index = row_owner * capacity + jnp.sum(same_owner.astype(jnp.int32), axis=1)
    dispatch = slot_index[:, None] == jnp.arange(slot_count, dtype=jnp.int32)[None, :]
    slot_used = jnp.any(dispatch, axis=0)
    slot_row = jnp.sum(jnp.where(dispatch, row_iota[:, None], 0), axis=0)

    def to_slots(rows_data):
        picked = jnp.take(rows_data, slot_row, axis=0)
        mask_shape = (slot_count,) + (1,) * (rows_data.ndim - 1)
        picked = jnp.where(slot_used.reshape(mask_shape), picked, jnp.zeros_like(picked))
        return picked.reshape((peer_count, capacity) + rows_data.shape[1:])

    live_len = jnp.where(finished == 1, resp_len, 0).astype(jnp.bfloat16)
    own_all = jnp.concatenate([resp_cache, new_kv], axis=1)
    reply_iota = jnp.arange(resp_slots + step_count)
    pol_keys = policy_prompt[0, :, 0].reshape(prompt_width, kv_heads, HD)
    pol_values = policy_prompt[0, :, 1].reshape(prompt_width, kv_heads, HD)
    prompt_valid = jnp.arange(prompt_width) < prompt_len[0]
    resp_keys = own_all[:, :, 0].reshape(row_count, -1, kv_heads, HD)
    resp_values = own_all[:, :, 1].reshape(row_count, -1, kv_heads, HD)
    previous = jnp.zeros((row_count, q_width), jnp.float32)
    decoded_list = []
    kept_list = []
    for step_idx in range(step_count):
        queries = (step_input[:, step_idx].astype(jnp.float32) + previous).astype(jnp.bfloat16)
        received = lax.all_to_all(to_slots(queries), "dp", split_axis=0, concat_axis=0, tiled=True)
        lead_shape = received.shape[:2]
        prompt_queries = received.reshape(-1, kv_heads, group_size, HD)
        scores = (
            jnp.einsum(
                "skgd,tkd->skgt", prompt_queries, pol_keys, preferred_element_type=jnp.float32
            )
            * inv_scale
        )
        prompt_weight, prompt_weight_sum, prompt_top_score = softmax_pieces(scores, prompt_valid)
        prompt_summed = jnp.einsum(
            "skgt,tkd->skgd",
            prompt_weight.astype(jnp.bfloat16),
            pol_values,
            preferred_element_type=jnp.float32,
        )
        part_out = (
            (prompt_summed / prompt_weight_sum[..., None])
            .astype(jnp.bfloat16)
            .reshape(lead_shape + (q_width,))
        )
        part_lse = (prompt_top_score + jnp.log(prompt_weight_sum)).reshape(lead_shape + (q_heads,))
        back_out = lax.all_to_all(part_out, "dp", split_axis=0, concat_axis=0, tiled=True)
        back_lse = lax.all_to_all(part_lse, "dp", split_axis=0, concat_axis=0, tiled=True)
        results = (back_out, back_lse, received)
        back_out = results[0]
        back_lse = results[1]
        kept_list.append(results[2])
        prompt_out = jnp.take(back_out.reshape(slot_count, q_width), slot_index, axis=0).astype(
            jnp.float32
        )
        prompt_lse = jnp.take(back_lse.reshape(slot_count, q_heads), slot_index, axis=0)
        query_heads = queries.reshape(row_count, kv_heads, group_size, HD)
        scores = (
            jnp.einsum(
                "rkgd,rtkd->rkgt", query_heads, resp_keys, preferred_element_type=jnp.float32
            )
            * inv_scale
        )
        reply_valid = jnp.where(
            reply_iota[None, :] < resp_slots,
            reply_iota[None, :] < resp_len[:, None],
            reply_iota[None, :] <= resp_slots + step_idx,
        )
        weight, weight_sum, top_score = softmax_pieces(scores, reply_valid[:, None, None, :])
        summed = jnp.einsum(
            "rkgt,rtkd->rkgd",
            weight.astype(jnp.bfloat16),
            resp_values,
            preferred_element_type=jnp.float32,
        )
        own_out = (summed / weight_sum[..., None]).reshape(row_count, q_heads, HD)
        own_lse = (top_score + jnp.log(weight_sum)).reshape(row_count, q_heads)
        joint_lse = jnp.maximum(prompt_lse, own_lse)
        prompt_wt = jnp.exp(prompt_lse - joint_lse)
        own_wt = jnp.exp(own_lse - joint_lse)
        blended = (
            prompt_wt[..., None] * prompt_out.reshape(row_count, q_heads, HD)
            + own_wt[..., None] * own_out
        ) / (prompt_wt + own_wt)[..., None]
        decoded_now = blended.reshape(row_count, q_width).astype(jnp.bfloat16)
        decoded_list.append(decoded_now)
        previous = lax.optimization_barrier(decoded_now).astype(jnp.float32)
    recv_kv, recv_live = (
        lax.all_to_all(to_slots(own_all), "dp", split_axis=0, concat_axis=0, tiled=True),
        lax.all_to_all(to_slots(live_len), "dp", split_axis=0, concat_axis=0, tiled=True),
    )
    recv_queries = jnp.stack(kept_list, axis=2)
    ref_keys = ref_prompt[0, :, 0].reshape(prompt_width, kv_heads, HD)
    ref_values = ref_prompt[0, :, 1].reshape(prompt_width, kv_heads, HD)
    slot_kv = recv_kv.reshape(slot_count, resp_slots + step_count, 2, kv_width)
    slot_keys = slot_kv[:, :, 0].reshape(slot_count, -1, kv_heads, HD)
    slot_values = slot_kv[:, :, 1].reshape(slot_count, -1, kv_heads, HD)
    slot_len = recv_live.reshape(slot_count).astype(jnp.int32)
    slot_queries = recv_queries.reshape(slot_count, step_count, q_width)
    probe_heads = probe.reshape(kv_heads, group_size, HD)
    prompt_mask = jnp.broadcast_to(prompt_valid[None, :], (slot_count, prompt_width))
    score_list = []
    for step_idx in range(step_count):
        queries = slot_queries[:, step_idx].reshape(slot_count, kv_heads, group_size, HD)
        prompt_scores = (
            jnp.einsum("skgd,tkd->skgt", queries, ref_keys, preferred_element_type=jnp.float32)
            * inv_scale
        )
        reply_scores = (
            jnp.einsum("skgd,stkd->skgt", queries, slot_keys, preferred_element_type=jnp.float32)
            * inv_scale
        )
        reply_valid = jnp.where(
            reply_iota[None, :] < resp_slots,
            reply_iota[None, :] < slot_len[:, None],
            reply_iota[None, :] <= resp_slots + step_idx,
        )
        key_valid = jnp.concatenate([prompt_mask, reply_valid], axis=1)
        weight, weight_sum, top_score = softmax_pieces(
            jnp.concatenate([prompt_scores, reply_scores], axis=-1), key_valid[:, None, None, :]
        )
        weight_low = weight.astype(jnp.bfloat16)
        summed = jnp.einsum(
            "skgt,tkd->skgd",
            weight_low[..., :prompt_width],
            ref_values,
            preferred_element_type=jnp.float32,
        )
        summed = summed + jnp.einsum(
            "skgt,stkd->skgd",
            weight_low[..., prompt_width:],
            slot_values,
            preferred_element_type=jnp.float32,
        )
        ref_out = summed / weight_sum[..., None]
        score_list.append(
            jnp.einsum("skgd,kgd->s", ref_out, probe_heads, precision=lax.Precision.HIGHEST)
        )
    head_terms = jnp.stack(score_list, axis=1)
    head_total = lax.psum(head_terms, "tensor")
    ref_score = jnp.where(slot_len[:, None] > 0, head_total, jnp.zeros((), jnp.float32)).reshape(
        1, slot_count, step_count
    )
    return (jnp.stack(decoded_list, axis=1), ref_score)


def ring_order(count):
    return list(range(0, count, 2)) + list(range(count - 1, 0, -2))


def ring_owner(me, nth, count):
    half = lax.div(me, 2)
    spot = jnp.where(lax.rem(me, 2) == 0, half, count - 1 - half)
    step = (nth + 1) // 2
    spot = lax.rem(spot + (step if nth % 2 == 0 else count - step), count)
    return jnp.where(spot < count // 2, 2 * spot, 2 * (count - 1 - spot) + 1)


def iota(shape, dim):
    return lax.broadcasted_iota(jnp.int32, shape, dim)


def split_matrix(pairs):
    i = iota((2 * pairs, 2 * pairs), 0)
    j = iota((2 * pairs, 2 * pairs), 1)
    src = jnp.where(i < pairs, 2 * i, 2 * (i - pairs) + 1)
    return jnp.where(src == j, 1.0, 0.0).astype(jnp.bfloat16)


def swap_matrix(outer, inner):
    n = outer * inner
    i = iota((n, n), 0)
    j = iota((n, n), 1)
    src = (i % outer) * inner + i // outer
    return jnp.where(src == j, 1.0, 0.0).astype(jnp.bfloat16)


def mm(a, b):
    return jnp.dot(a, b, preferred_element_type=jnp.float32)


def mm_t(a, b):
    return lax.dot_general(a, b, (((1,), (1,)), ((), ())), preferred_element_type=jnp.float32)


def slots_kernel(me_ref, owner_ref, len_ref, fin_ref, slot_ref, count_ref):
    peers = count_ref.shape[0]
    slots = slot_ref.shape[1]
    slot_ref[3, 0] = me_ref[0]
    capacity = slots // peers
    for i in range(slots):
        slot_ref[0, i] = -1
        slot_ref[1, i] = 1
        slot_ref[2, i] = 0
    for o in range(peers):
        count_ref[o] = 0

    def place(r, c):
        o = jnp.clip(owner_ref[r], 0, peers - 1)
        k = count_ref[o]
        at = o * capacity + jnp.minimum(k, capacity - 1)
        slot_ref[0, at] = r
        slot_ref[1, at] = len_ref[r]
        slot_ref[2, at] = fin_ref[r]
        count_ref[o] = k + 1
        return c

    lax.fori_loop(0, owner_ref.shape[0], place, 0, unroll=4)


def slot_tables(me, row_owner, resp_len, finished, peers, capacity):
    smem = pl.BlockSpec(memory_space=pltpu.SMEM)
    return pl.pallas_call(
        slots_kernel,
        in_specs=[smem] * 4,
        out_specs=smem,
        out_shape=jax.ShapeDtypeStruct((4, peers * capacity), jnp.int32),
        scratch_shapes=[pltpu.SMEM((peers,), jnp.int32)],
        name="slots",
    )(me, row_owner, resp_len, finished)


def own_masks(slot_ref, base, rows, old, steps, width):
    lane = iota((rows, width), 1)
    sub = iota((rows, width), 0)
    split = rows * old
    is_old = lane < split
    key_row = jnp.where(is_old, lane // old, (lane - split) // steps)
    key_pos = jnp.where(is_old, lane % old, (lane - split) % steps)
    limit = jnp.zeros((rows, width), jnp.int32)
    for k in range(rows):
        limit = jnp.where(sub == k, slot_ref[1, base + k], limit)
    mine = (key_row == sub) & (lane < rows * (old + steps))
    return [
        mine & (key_pos < jnp.where(is_old, limit, step_idx + 1)) for step_idx in range(steps)
    ]


def make_work(peers, pieces, begin, last, earlier, capacity, steps, old, kv_heads, group):
    head_rows = group * capacity
    inv_scale = 1.0 / math.sqrt(HD)
    n_old, n_new = capacity * old, capacity * steps

    def body(*refs):
        refs = list(refs)
        slot_ref, x_hbm, rc_hbm, nk_hbm, probe_hbm = refs[:5]
        refs = refs[5:]
        pols, refs = refs[:pieces], refs[pieces:]
        rfs, refs = refs[:pieces], refs[pieces:]
        if begin > 0:
            refs = refs[1:]
        olds, refs = refs[:earlier], refs[earlier:]
        dec_hbm, score_ref = refs[:2]
        probe_ref, polbuf, refbuf, xbuf, rcbuf, nkbuf, xs, kc, vc, qs, obuf, insem, rowsem, outsem, probesem = refs[2:]
        width = kc.shape[1] // 3
        kv_width = kv_heads * HD
        me = slot_ref[3, 0]
        owners = [ring_owner(me, begin + p, peers) for p in range(pieces)]
        loads, flights = [], []
        for p in range(pieces):
            flight = []
            for k in range(capacity):
                row = jnp.maximum(slot_ref[0, owners[p] * capacity + k], 0)
                flight += [
                    pltpu.make_async_copy(x_hbm.at[row], xbuf.at[p, k], rowsem.at[p, k, 0]),
                    pltpu.make_async_copy(rc_hbm.at[row], rcbuf.at[p, k], rowsem.at[p, k, 1]),
                    pltpu.make_async_copy(nk_hbm.at[row], nkbuf.at[p, k], rowsem.at[p, k, 2]),
                ]
            flights.append(flight)
            loads.append(
                [
                    pltpu.make_async_copy(pols[p].at[0], polbuf.at[p], insem.at[p, 0]),
                    pltpu.make_async_copy(rfs[p].at[0], refbuf.at[p], insem.at[p, 1]),
                ]
            )
        for p in range(pieces):
            for c in flights[p] + loads[p]:
                c.start()
        probe_load = pltpu.make_async_copy(probe_hbm, probe_ref, probesem)
        probe_load.start()
        split_p = split_matrix(width)
        split_rc = split_matrix(n_old)
        split_nk = split_matrix(n_new)
        to_steps = swap_matrix(capacity, steps)
        to_rows = swap_matrix(steps, capacity)
        masks = [
            own_masks(slot_ref, owners[p] * capacity, capacity, old, steps, width)
            for p in range(pieces)
        ]
        lane = iota((capacity, width), 1).astype(jnp.float32)
        zero = jnp.zeros((width - n_old - n_new, kv_width), jnp.float32)
        pmask = []
        for p in range(pieces):
            for c in flights[p]:
                c.wait()
            rc = mm(split_rc, rcbuf[p].reshape(2 * n_old, kv_width))
            nk = mm(split_nk, nkbuf[p].reshape(2 * n_new, kv_width))
            own_k = jnp.concatenate([rc[:n_old], nk[:n_new], zero], 0).astype(jnp.bfloat16)
            own_v = jnp.concatenate([rc[n_old:], nk[n_new:], zero], 0).astype(jnp.bfloat16)
            kc[p, width : 2 * width] = own_k
            vc[p, width : 2 * width] = own_v
            xs[p] = mm(to_steps, xbuf[p].reshape(n_new, -1))
            for c in loads[p]:
                c.wait()
            both = mm(split_p, polbuf[p].reshape(2 * width, kv_width)).astype(jnp.bfloat16)
            kc[p, :width] = both[:width]
            vc[p, :width] = both[width:]
            both = mm(split_p, refbuf[p, :width].reshape(2 * width, kv_width)).astype(jnp.bfloat16)
            kc[p, 2 * width :] = both[:width]
            vc[p, 2 * width :] = both[width:]
            length = refbuf[p, width].astype(jnp.float32)[:1, :width]
            pmask.append(jnp.concatenate([lane < length] * group, 0))
        prev = [[None] * kv_heads for _ in range(pieces)]
        done = [[None] * steps for _ in range(pieces)]
        for s in range(steps):
            for p in range(pieces):
                omask = jnp.concatenate([masks[p][s]] * group, 0)
                parts = []
                for g in range(kv_heads):
                    at = slice(g * HD, (g + 1) * HD)
                    q = jnp.concatenate(
                        [
                            xs[p, s * capacity : (s + 1) * capacity, (g * group + h) * HD : (g * group + h + 1) * HD]
                            for h in range(group)
                        ],
                        0,
                    )
                    if s > 0:
                        q = q + prev[p][g]
                    q = q.astype(jnp.bfloat16)
                    qs[p, g, s * head_rows : (s + 1) * head_rows] = q
                    z = mm_t(q, kc[p, : 2 * width, at]) * inv_scale
                    zp = jnp.where(pmask[p], z[:, :width], -jnp.inf)
                    zo = jnp.where(omask, z[:, width:], -jnp.inf)
                    top_p = jnp.max(zp, axis=1, keepdims=True)
                    top_o = jnp.max(zo, axis=1, keepdims=True)
                    wp = jnp.exp(zp - top_p)
                    wo = jnp.exp(zo - top_o)
                    lp = jnp.sum(wp, axis=1, keepdims=True)
                    lo = jnp.sum(wo, axis=1, keepdims=True)
                    accp = mm(wp.astype(jnp.bfloat16), vc[p, :width, at])
                    acco = mm(wo.astype(jnp.bfloat16), vc[p, width : 2 * width, at])
                    out_p = (accp * (1.0 / lp)).astype(jnp.bfloat16).astype(jnp.float32)
                    top = jnp.maximum(top_p, top_o)
                    a = lp * jnp.exp(top_p - top)
                    c = jnp.exp(top_o - top)
                    inv = 1.0 / (a + lo * c)
                    mix = out_p * (a * inv) + acco * (c * inv)
                    mix = mix.astype(jnp.bfloat16).astype(jnp.float32)
                    prev[p][g] = mix
                    parts += [mix[h * capacity : (h + 1) * capacity] for h in range(group)]
                done[p][s] = jnp.concatenate(parts, 1)
        for p in range(pieces):
            d = jnp.concatenate(done[p], 0).astype(jnp.bfloat16)
            obuf[p] = mm(to_rows, d).astype(jnp.bfloat16).reshape(obuf.shape[1:])
            for k in range(capacity):
                row = slot_ref[0, owners[p] * capacity + k]

                @pl.when(row >= 0)
                def _():
                    pltpu.make_async_copy(obuf.at[p, k], dec_hbm.at[row], outsem.at[p, k]).start()

        probe_load.wait()
        out_lane = iota((capacity, HD), 1)
        out_sub = iota((capacity, HD), 0)
        for p in range(pieces):
            full = jnp.concatenate(
                [
                    jnp.concatenate([jnp.concatenate([masks[p][s]] * group, 0), pmask[p]], 1)
                    for s in range(steps)
                ],
                0,
            )
            total = [jnp.zeros((capacity, HD), jnp.float32) for _ in range(steps)]
            for g in range(kv_heads):
                at = slice(g * HD, (g + 1) * HD)
                z = mm_t(qs[p, g], kc[p, width:, at]) * inv_scale
                z = jnp.where(full, z, -jnp.inf)
                w = jnp.exp(z - jnp.max(z, axis=1, keepdims=True))
                acc = mm(w.astype(jnp.bfloat16), vc[p, width:, at])
                acc = acc * (1.0 / jnp.sum(w, axis=1, keepdims=True))
                for s in range(steps):
                    for h in range(group):
                        lo = (s * group + h) * capacity
                        weight = probe_ref[g * group + h : g * group + h + 1, :]
                        total[s] = total[s] + acc[lo : lo + capacity] * weight
            live = jnp.zeros((capacity, HD), jnp.int32)
            for k in range(capacity):
                live = jnp.where(out_sub == k, slot_ref[2, owners[p] * capacity + k], live)
            here = (out_lane == me * capacity + out_sub) & (live == 1)
            rows = []
            for s in range(steps):
                value = jnp.sum(total[s], axis=1, keepdims=True)
                rows.append(jnp.sum(jnp.where(here, value, 0.0), axis=0, keepdims=True))
            rows = jnp.concatenate(rows, 0)
            if last:
                for t in range(score_ref.shape[1]):
                    score_ref[owners[p], t] = rows
            else:
                score_ref[p] = rows
        if last:
            n = 0
            for part in olds:
                for i in range(part.shape[0]):
                    for t in range(score_ref.shape[1]):
                        score_ref[ring_owner(me, n, peers), t] = part[i]
                    n += 1
        for p in range(pieces):
            for k in range(capacity):
                row = slot_ref[0, owners[p] * capacity + k]

                @pl.when(row >= 0)
                def _():
                    pltpu.make_async_copy(obuf.at[p, k], dec_hbm.at[row], outsem.at[p, k]).wait()

    return body


def work_pieces(peers, slots, rows, probe, pols, rfs, dec, olds, begin, last, halves):
    x, rc, _ = rows
    pieces = len(pols)
    _, steps, q_width = x.shape
    _, width, _, kv_width = pols[0].shape
    old = rc.shape[1]
    capacity = slots.shape[1] // peers
    kv_heads = kv_width // HD
    group = q_width // kv_width
    body = make_work(peers, pieces, begin, last, len(olds), capacity, steps, old, kv_heads, group)
    smem = pl.BlockSpec(memory_space=pltpu.SMEM)
    vmem = pl.BlockSpec(memory_space=pltpu.VMEM)
    anyspec = pl.BlockSpec(memory_space=pltpu.HBM)
    big = [pltpu.with_memory_space_constraint(v, pltpu.HBM) for v in (*rows, probe)]
    if begin == 0:
        pols = [pltpu.with_memory_space_constraint(v, pltpu.HBM) for v in pols]
    big += [*pols, *rfs]
    args = [slots, *big]
    specs = [smem] + [anyspec] * len(big)
    alias = {}
    if begin > 0:
        alias = {len(args): 0}
        args.append(dec)
        specs.append(anyspec)
    args += olds
    specs += [vmem] * len(olds)
    bf = jnp.bfloat16
    scores = (peers, halves, steps, HD) if last else (pieces, steps, HD)
    return pl.pallas_call(
        body,
        in_specs=specs,
        out_specs=[anyspec, vmem],
        out_shape=[
            jax.ShapeDtypeStruct(x.shape, bf),
            jax.ShapeDtypeStruct(scores, jnp.float32),
        ],
        scratch_shapes=[
            pltpu.VMEM(probe.shape, jnp.float32),
            pltpu.VMEM((pieces, width, 2, kv_width), bf),
            pltpu.VMEM((pieces, width + 1, 2, kv_width), bf),
            pltpu.VMEM((pieces, capacity, steps, q_width), bf),
            pltpu.VMEM((pieces, capacity, old, 2, kv_width), bf),
            pltpu.VMEM((pieces, capacity, steps, 2, kv_width), bf),
            pltpu.VMEM((pieces, capacity * steps, q_width), jnp.float32),
            pltpu.VMEM((pieces, 3 * width, kv_width), bf),
            pltpu.VMEM((pieces, 3 * width, kv_width), bf),
            pltpu.VMEM((pieces, kv_heads, steps * group * capacity, HD), bf),
            pltpu.VMEM((pieces, capacity, steps, q_width), bf),
            pltpu.SemaphoreType.DMA((pieces, 2)),
            pltpu.SemaphoreType.DMA((pieces, capacity, 3)),
            pltpu.SemaphoreType.DMA((pieces, capacity)),
            pltpu.SemaphoreType.DMA,
        ],
        input_output_aliases=alias,
        compiler_params=pltpu.CompilerParams(vmem_limit_bytes=24 << 20),
        cost_estimate=pl.CostEstimate(flops=0, transcendentals=0, bytes_accessed=16 << 20),
        name="work",
    )(*args)


def ring_fits(step_input, new_kv, resp_cache, policy_prompt, *rest):
    peers = lax.axis_size("dp")
    row_count, step_count, q_width = step_input.shape
    old = resp_cache.shape[1]
    kv_width = new_kv.shape[3]
    width = policy_prompt.shape[1]
    capacity = max(2, (row_count + peers - 1) // peers)
    gathered = 2 * peers * policy_prompt.size
    exchanged = 2 * step_input.size + new_kv.size + resp_cache.size
    return (
        gathered <= exchanged
        and peers % 2 == 0
        and peers >= 4
        and capacity % 8 == 0
        and peers * capacity <= HD
        and capacity * (old + step_count) <= width
        and width % HD == 0
        and q_width % kv_width == 0
    )


def per_device_ring(
    step_input,
    new_kv,
    resp_cache,
    policy_prompt,
    ref_prompt,
    prompt_len,
    resp_len,
    row_owner,
    finished,
    probe,
):
    row_count, step_count, q_width = step_input.shape
    peers = lax.axis_size("dp")
    halves = lax.axis_size("tensor")
    capacity = max(2, (row_count + peers - 1) // peers)
    ring = ring_order(peers)
    forward = [(ring[i], ring[(i + 1) % peers]) for i in range(peers)]
    backward = [(b, a) for a, b in forward]
    me = lax.axis_index("dp").astype(jnp.int32).reshape(1)
    probe_heads = probe.reshape(q_width // HD, HD)

    def hop(value, pairs):
        return lax.ppermute(value, "dp", pairs)

    pf = hop(policy_prompt, forward)
    pb = hop(policy_prompt, backward)
    mark = jnp.broadcast_to(prompt_len.astype(jnp.bfloat16), (1, 1) + ref_prompt.shape[2:])
    ref0 = jnp.concatenate([ref_prompt, mark], axis=1)
    rf = hop(ref0, forward)
    rb = hop(ref0, backward)
    slots = slot_tables(me, row_owner, resp_len, finished, peers, capacity)
    rows = (step_input, resp_cache, new_kv)

    def work(pols, rfs, dec, olds, begin, last=False):
        return work_pieces(
            peers, slots, rows, probe_heads, pols, rfs, dec, olds, begin, last, halves
        )

    dec, score = work([policy_prompt], [ref0], None, [], 0)
    scores = [score]
    begin = 1
    for d in range(1, peers // 2):
        now = [pf, pb], [rf, rb]
        pf = hop(pf, forward)
        if d + 1 < peers // 2:
            pb = hop(pb, backward)
            rf = hop(rf, forward)
        rb = hop(rb, backward)
        dec, score = work(*now, dec, [], begin)
        scores.append(score)
        begin += len(now[0])
    dec, send = work([pf], [rb], dec, scores, begin, True)
    got = lax.all_to_all(
        send.reshape(peers * halves, step_count, HD),
        ("dp", "tensor"),
        split_axis=0,
        concat_axis=0,
        tiled=True,
    )
    total = jnp.sum(got, axis=0)[:, : peers * capacity]
    return dec, total.T.reshape(1, peers * capacity, step_count)


def solution(mesh):
    in_specs = (
        P(("groups", "dp"), None, "tensor"),
        P(("groups", "dp"), None, None, "tensor"),
        P(("groups", "dp"), None, None, "tensor"),
        P(("groups", "dp"), None, None, "tensor"),
        P(("groups", "dp"), None, None, "tensor"),
        P(("groups", "dp")),
        P(("groups", "dp")),
        P(("groups", "dp")),
        P(("groups", "dp")),
        P("tensor"),
    )
    out_specs = (P(("groups", "dp"), None, "tensor"), P(("groups", "dp"), None, None))

    def run(*args):
        return per_device_ring(*args) if ring_fits(*args) else per_device(*args)

    return jax.shard_map(
        run, mesh=mesh, in_specs=in_specs, out_specs=out_specs, check_vma=False
    )
```
